128 devices in a mesh: wide: 8 (over y, core), narrow: 16 (over z, x).
Axes of the slice: x: 4, y: 4, z: 4, core: 2. Of those that a mesh axis runs over, the one named last changes fastest.
Arguments:
- latent_in: bfloat16 [2048, 1024], P(('wide', 'narrow')), may hold values from -6 to 6
- latent_grad: bfloat16 [2048, 1024], P(('wide', 'narrow')), may hold values from -6 to 6
- route_ids: int32 [2048, 22], P(('wide', 'narrow')), may hold values from 0 to 127, all different within a row; in each aligned block of 16 rows (0 to 15, 16 to 31, ...) at most 8 rows name the same one
- gate_values: float32 [2048, 22], P(('wide', 'narrow')), may hold values from 0.05 to 1
- up_weight: bfloat16 [128, 1024, 2688], P(('wide', 'narrow')), may hold values from -0.1875 to 0.1875
- down_weight: bfloat16 [128, 2688, 1024], P(('wide', 'narrow')), may hold values from -0.125 to 0.125
- inputs: bfloat16 [2048, 4096], P('wide', 'narrow'), may hold values from -6 to 6
- proj_weight: bfloat16 [4096, 1024], P('narrow'), may hold values from -0.09375 to 0.09375
Outputs:
- grad_up: bfloat16 [128, 1024, 2688], P(('wide', 'narrow'))
- grad_down: bfloat16 [128, 2688, 1024], P(('wide', 'narrow'))
- grad_inputs: bfloat16 [2048, 4096], P('wide', 'narrow')
- grad_proj: float32 [4096, 1024], P('narrow', 'wide')
The draws below stay inside these ranges and needn't reach their ends.
Inputs may be any that keep to these rules, and one draw needn't show every extreme that they name: `route_ids`: each token names 22 different experts; among the 16 tokens of one device no expert is named by more than 8 tokens, a bound that some block reaches.
All inputs are finite; a program needn't handle non-finite values.
Results may differ from the reference program's by a relative error of at most 0.015.
Values may be sent and summed in bfloat16 or wider, within the bound.
No kernel may reach another device: no remote copies, remote signals or barrier semaphores. Data moves between devices by JAX's collectives and lax.ppermute only.
A program may use at most 128 MiB of HBM per device.

```python
import math
import jax
import jax.numpy as jnp
import numpy as np
from jax import lax

D = 4096
L = 1024
FF = 2688
TOPK = 22
TOK_DEV = 16
EXPERTS = 128
CAP = 8
TOKENS = 2048
N_WIDE = 8
N_NARROW = 16


def level_of(rng, shape, cuts, smallest, top_value):
    def one(axis_at, shards_of):
        steps = jax.random.uniform(jax.random.fold_in(jax.random.fold_in(rng, 6), axis_at), (shards_of,), jnp.float32, smallest / len(cuts), top_value / len(cuts))
        return jnp.repeat(jnp.exp(steps), shape[axis_at] // shards_of).reshape((-1,) + (1,) * (len(shape) - axis_at - 1))

    level = one(*cuts[0])
    for cut in cuts[1:]:
        level = level * one(*cut)
    return level


def routed_block(own_key, own, number, rows, count, top, limit, skew):
    sequence = jax.random.permutation(own_key, count)
    heavy_load, common = portions_of(count, rows * top, limit, skew, True), portions_of(count, rows * top, limit, skew, False)
    places = jnp.arange(count)

    def named(tallies, offset_by):
        used = int((tallies > 0).sum())
        fixed = max(1, used // 4)
        shifted = fixed + (places - fixed + offset_by * (used - fixed)) % max(1, count - fixed)
        return jnp.zeros((count,), jnp.int32).at[sequence[jnp.where(places < fixed, places, shifted)]].set(jnp.asarray(tallies, jnp.int32))

    tallies = jnp.where(number % 4 == 0, named(heavy_load, number // 4), named(common, number - number // 4 - 1))
    mixed = jax.random.permutation(jax.random.fold_in(own, 3), count)
    source_of, receiver = mixed[0:count // 2 * 2:2], mixed[1:count // 2 * 2:2]
    margin = jnp.minimum(tallies[source_of] - 1, limit - tallies[receiver]) // 2
    margin = jnp.where((source_of == sequence[0]) | (receiver == sequence[0]) | (tallies[receiver] == 0), 0, jnp.maximum(margin, 0))
    shifted = jax.random.randint(jax.random.fold_in(own, 4), (count // 2,), 0, 1 << 20) % (margin + 1)
    tallies = tallies.at[source_of].add(-shifted).at[receiver].add(shifted)
    labels = jnp.searchsorted(jnp.cumsum(tallies), jnp.arange(rows * top), side="right").astype(jnp.int32)
    grid = labels.reshape(top, rows).T
    grid = grid[jax.random.permutation(jax.random.fold_in(own, 1), rows)]
    offset_by = jax.random.randint(jax.random.fold_in(own, 2), (rows, 1), 0, top)
    return jnp.take_along_axis(grid, (jnp.arange(top)[None, :] + offset_by) % top, axis=1)


def portions_of(number_of, total, most, lean, full):
    loads = [(1 << 20) // math.isqrt(grade ** lean) + 1 for grade in range(1, number_of + 1)]
    largest = most if full else min(most, max(-(-total // number_of), total * loads[0] // sum(loads)))
    least = 1 if total - largest >= number_of - 1 else 0
    given, rest = [largest] + [least] * (number_of - 1), total - largest - least * (number_of - 1)
    while rest > 0:
        candidates = [i for i in range(1, number_of) if given[i] < largest] or [i for i in range(1, number_of) if given[i] < most]
        pool, left = sum([loads[i] for i in candidates]), rest
        for i in candidates:
            addition = min(most - given[i], max(1, left * loads[i] // pool), rest)
            given[i] = given[i] + addition
            rest = rest - addition
    return np.array(given)


def normal_values(key, shape, scale, bound, pieces=(), kind=jnp.bfloat16):
    entries = jax.random.normal(key, shape, jnp.float32) * scale
    if len(pieces) > 0:
        entries = level_of(key, shape, pieces, -0.22, 0.18) * entries
    return jnp.clip(entries, min=-bound, max=bound).astype(kind)


def setup_inputs(seed: int = 0) -> dict:
    streams_of = jax.random.split(jax.random.key(seed), 9)
    latent_in = normal_values(streams_of[0], (TOKENS, L), 1.0, 6.0, ((0, 128),))
    latent_grad = normal_values(streams_of[1], (TOKENS, L), 1.0, 6.0, ((0, 128),))
    route_ids_keys = jax.random.split(jax.random.fold_in(streams_of[2], 1), TOKENS // TOK_DEV)
    route_ids_turns = jax.random.permutation(jax.random.fold_in(streams_of[2], 3), TOKENS // TOK_DEV)
    route_ids = jax.vmap(lambda own, number: routed_block(jax.random.fold_in(streams_of[2], 2), own, number, TOK_DEV, EXPERTS, TOPK, CAP, 2))(route_ids_keys, route_ids_turns).reshape((TOKENS, TOPK))
    gate_values = jnp.clip(0.05 + 0.95 * jax.random.uniform(streams_of[3], (TOKENS, TOPK), jnp.float32) ** level_of(streams_of[3], (TOKENS, TOPK), ((0, 128),), -0.2, 0.2), 0.05, 1.0)
    up_weight = normal_values(streams_of[4], (EXPERTS, L, FF), L ** -0.5, 0.1875, ((0, 128),))
    down_weight = normal_values(streams_of[5], (EXPERTS, FF, L), FF ** -0.5, 0.125, ((0, 128),))
    inputs = normal_values(streams_of[6], (TOKENS, D), 1.0, 6.0, ((0, 8), (1, 16)))
    proj_weight = normal_values(streams_of[7], (D, L), D ** -0.5, 0.09375, ((0, 16),))
    return {"latent_in": latent_in, "latent_grad": latent_grad, "route_ids": route_ids, "gate_values": gate_values, "up_weight": up_weight, "down_weight": down_weight, "inputs": inputs, "proj_weight": proj_weight}


def expert_pass(z_rows, dy_rows, w_up, w_down):
    hidden = jnp.dot(z_rows, w_up, preferred_element_type=jnp.float32)
    active = jnp.maximum(hidden, 0.0)
    squared = (active * active).astype(jnp.bfloat16)
    act_grad = lax.dot_general(dy_rows, w_down, (((1,), (1,)), ((), ())), preferred_element_type=jnp.float32)
    hid_grad = (act_grad * 2.0 * active).astype(jnp.bfloat16)
    row_grad = lax.dot_general(hid_grad, w_up, (((1,), (1,)), ((), ())), preferred_element_type=jnp.float32).astype(jnp.bfloat16)
    down_part = lax.dot_general(squared, dy_rows, (((0,), (0,)), ((), ())), preferred_element_type=jnp.float32)
    up_part = lax.dot_general(z_rows, hid_grad, (((0,), (0,)), ((), ())), preferred_element_type=jnp.float32)
    return row_grad, up_part, down_part


def reference(latent_in, latent_grad, route_ids, gate_values, up_weight, down_weight, inputs, proj_weight):
    experts = up_weight.shape[0]
    width = latent_in.shape[1]
    hidden_units = up_weight.shape[2]
    token_count = route_ids.shape[0]
    flat_routes = route_ids.reshape(-1).astype(jnp.int32)
    pairs = flat_routes.shape[0]
    block_rows = N_WIDE * N_NARROW
    bucket = CAP * block_rows
    order = jnp.argsort(flat_routes, stable=True).astype(jnp.int32)
    counts = jnp.sum((flat_routes[:, None] == jnp.arange(experts, dtype=jnp.int32)[None, :]).astype(jnp.int32), axis=0)
    starts = (jnp.cumsum(counts) - counts).astype(jnp.int32)
    order_pad = jnp.concatenate([order, jnp.full((bucket,), pairs, jnp.int32)])
    token_pad = jnp.concatenate([jnp.arange(pairs, dtype=jnp.int32) // TOPK, jnp.full((1,), token_count, jnp.int32)])
    gate_pad = jnp.concatenate([gate_values.reshape(-1).astype(jnp.float32), jnp.zeros((1,), jnp.float32)])
    empty_row = jnp.zeros((1, width), jnp.bfloat16)
    z_pad = jnp.concatenate([latent_in, empty_row])
    dy_pad = jnp.concatenate([latent_grad, empty_row])

    def one_expert(expert_id):
        count_here = counts[expert_id]
        pair_index = lax.dynamic_slice_in_dim(order_pad, starts[expert_id], bucket)
        live = jnp.arange(bucket, dtype=jnp.int32) < count_here
        pair_index = jnp.where(live, pair_index, pairs).astype(jnp.int32)
        token_index = token_pad[pair_index]
        z_rows = z_pad[token_index]
        dy_rows = (dy_pad[token_index].astype(jnp.float32) * gate_pad[pair_index][:, None]).astype(jnp.bfloat16)
        w_up = up_weight[expert_id]
        w_down = down_weight[expert_id]

        def turn_step(turn, carry):
            first = (turn * block_rows).astype(jnp.int32)

            def do_work(state):
                up_acc, down_acc, rows_acc = state
                z_block = lax.dynamic_slice_in_dim(z_rows, first, block_rows, 0)
                dy_block = lax.dynamic_slice_in_dim(dy_rows, first, block_rows, 0)
                row_grad, up_part, down_part = expert_pass(z_block, dy_block, w_up, w_down)
                rows_acc = lax.dynamic_update_slice_in_dim(rows_acc, row_grad, first, 0)
                return (up_acc + up_part, down_acc + down_part, rows_acc)

            def skip_work(state):
                return state

            return lax.cond(first < count_here, do_work, skip_work, carry)

        start_state = (jnp.zeros((width, hidden_units), jnp.float32), jnp.zeros((hidden_units, width), jnp.float32), jnp.zeros((bucket, width), jnp.bfloat16))
        up_acc, down_acc, rows_acc = lax.fori_loop(0, CAP, turn_step, start_state)
        return up_acc.astype(jnp.bfloat16), down_acc.astype(jnp.bfloat16), rows_acc, pair_index

    grad_up, grad_down, rows_all, index_all = lax.map(one_expert, jnp.arange(experts, dtype=jnp.int32))
    pair_grads = jnp.zeros((pairs + 1, width), jnp.float32).at[index_all.reshape(-1)].set(rows_all.reshape(-1, width).astype(jnp.float32))[:pairs]
    token_grad = jnp.sum(pair_grads.reshape(token_count, TOPK, width), axis=1).astype(jnp.bfloat16)
    grad_inputs = lax.dot_general(token_grad, proj_weight, (((1,), (1,)), ((), ())), preferred_element_type=jnp.float32).astype(jnp.bfloat16)
    grad_proj = lax.dot_general(inputs, token_grad, (((0,), (0,)), ((), ())), preferred_element_type=jnp.float32)
    return grad_up, grad_down, grad_inputs, grad_proj
```

```python
import functools

import jax
import jax.numpy as jnp
from jax import lax
from jax.experimental import pallas as pl
from jax.experimental.pallas import tpu as pltpu
from jax.sharding import PartitionSpec as P

BF16 = jnp.bfloat16
F32 = jnp.float32
SLOTS = 8
PAD_MARK = 64.0
BLOCK = 512
VMEM_LIMIT = 56 * 1024 * 1024


def dot(a, b, dims, **kw):
    return lax.dot_general(a, b, (dims, ((), ())), preferred_element_type=F32, **kw)


NN = ((1,), (0,))
NT = ((1,), (1,))
TN = ((0,), (0,))


def pack_kernel(route_ref, gate_ref, z_ref, g_ref, send_ref, place_ref, *, rows):
    step = pl.program_id(0)
    tokens, top = route_ref.shape
    experts = 128
    width = z_ref.shape[1]
    routes = route_ref[...]
    gates = gate_ref[...]
    expert_of = lax.broadcasted_iota(jnp.int32, (tokens, experts), 1)
    hits = jnp.zeros((tokens, experts), F32)
    weights = jnp.zeros((tokens, experts), F32)
    for k in range(top):
        same = routes[:, k : k + 1] == expert_of
        hits = jnp.where(same, 1.0, hits)
        weights = jnp.where(same, gates[:, k : k + 1], weights)
    before = lax.broadcasted_iota(jnp.int32, (tokens, tokens), 1) < lax.broadcasted_iota(
        jnp.int32, (tokens, tokens), 0
    )
    rank = dot(before.astype(F32).astype(BF16), hits.astype(BF16), NN)
    rank = jnp.where(hits > 0, rank, -1.0).astype(BF16)
    row = lax.broadcasted_iota(jnp.int32, (rows, experts), 0)
    expert = lax.broadcasted_iota(jnp.int32, (rows, experts), 1)
    spread = jnp.where((row >> 3) + step * (rows // SLOTS) == expert, 1.0, 0.0)
    slot = lax.broadcasted_iota(jnp.int32, (rows, tokens), 0) & (SLOTS - 1)
    chosen = jnp.where(dot(spread.astype(BF16), rank, NT) == slot.astype(F32), 1.0, 0.0)
    gate = jnp.sum(
        chosen * dot(spread, weights, NT, precision=lax.Precision.HIGHEST), axis=1, keepdims=True
    )
    live = jnp.sum(chosen, axis=1, keepdims=True)
    chosen = chosen.astype(BF16)
    z_rows = dot(chosen, z_ref[...], NN)
    lane = lax.broadcasted_iota(jnp.int32, (rows, 128), 1)
    mark = jnp.where(lane == 0, (1.0 - live) * PAD_MARK, 0.0)
    send_ref[:, :128] = (z_rows[:, :128] + mark).astype(BF16)
    send_ref[:, 128:width] = z_rows[:, 128:].astype(BF16)
    send_ref[:, width:] = (dot(chosen, g_ref[...], NN) * gate).astype(BF16)
    slot_t = lax.broadcasted_iota(jnp.int32, (tokens, rows), 1) & (SLOTS - 1)
    place_ref[...] = jnp.where(
        dot(rank, spread.astype(BF16), NT) == slot_t.astype(F32), 1.0, 0.0
    ).astype(BF16)


def pack(routes, gates, z, g):
    tokens, width = z.shape
    total = 128 * SLOTS
    rows = 256
    whole = lambda a: pl.BlockSpec(a.shape, lambda i: (0, 0))
    return pl.pallas_call(
        functools.partial(pack_kernel, rows=rows),
        grid=(total // rows,),
        in_specs=[whole(routes), whole(gates), whole(z), whole(g)],
        out_specs=[
            pl.BlockSpec((rows, 2 * width), lambda i: (i, 0)),
            pl.BlockSpec((tokens, rows), lambda i: (0, i)),
        ],
        out_shape=[
            jax.ShapeDtypeStruct((total, 2 * width), BF16),
            jax.ShapeDtypeStruct((tokens, total), BF16),
        ],
        compiler_params=pltpu.CompilerParams(vmem_limit_bytes=VMEM_LIMIT),
        name="pack",
    )(routes, gates, z, g)


def chunks_of(hidden_units):
    edges = list(range(0, hidden_units, 768)) + [hidden_units]
    return list(zip(edges[:-1], edges[1:]))


def expert_kernel(
    recv_ref, up_hbm, down_hbm, ret_ref, zd_hbm, sq_hbm, hid_hbm, count_ref,
    up, down, zd, sq, hid, row_acc, row_out, pos_col, pos_row, in_sem, out_sem, zd_sem,
):
    total, twice = recv_ref.shape
    width = twice // 2
    chunks = chunks_of(up.shape[1])

    def weight_copies(n):
        a, b = chunks[n]
        return (
            pltpu.make_async_copy(up_hbm.at[:, a:b], up.at[:, a:b], in_sem.at[2 * n]),
            pltpu.make_async_copy(down_hbm.at[a:b, :], down.at[a:b, :], in_sem.at[2 * n + 1]),
        )

    def result_copies(i, n):
        a, b = chunks[n]
        r = slice(i * BLOCK, (i + 1) * BLOCK)
        return (
            pltpu.make_async_copy(sq.at[:, a:b], sq_hbm.at[r, a:b], out_sem.at[2 * n]),
            pltpu.make_async_copy(hid.at[:, a:b], hid_hbm.at[r, a:b], out_sem.at[2 * n + 1]),
        )

    def row_copy(i):
        return pltpu.make_async_copy(zd, zd_hbm.at[i * BLOCK : (i + 1) * BLOCK, :], zd_sem)

    for n in range(len(chunks)):
        for c in weight_copies(n):
            c.start()

    live = jnp.where(recv_ref[:, 0:128].astype(F32)[:, 0:1] < PAD_MARK / 2, 1.0, 0.0)
    live = jnp.broadcast_to(live, (total, 128))
    live_bf = live.astype(BF16)
    part = 256
    for p in range(total // part):
        r = slice(p * part, (p + 1) * part)
        earlier = (
            lax.broadcasted_iota(jnp.int32, (part, total), 1)
            < lax.broadcasted_iota(jnp.int32, (part, total), 0) + p * part
        )
        place = dot(jnp.where(earlier, 1.0, 0.0).astype(BF16), live_bf, NN)
        pos_col[r, :] = jnp.where(live[r, :] > 0, place, -1.0)
    pos_row[...] = pos_col[...].T
    count = jnp.max(pos_col[...]).astype(jnp.int32) + 1
    count_ref[0, 0] = count

    def one_block(i):
        want = (lax.broadcasted_iota(jnp.int32, (BLOCK, total), 0) + i * BLOCK).astype(F32)
        pick = jnp.where(jnp.broadcast_to(pos_row[0:1, :], (BLOCK, total)) == want, 1.0, 0.0)
        zd[...] = dot(pick.astype(BF16), recv_ref[...], NN).astype(BF16)
        row_copy(i).start()
        for n, (a, b) in enumerate(chunks):
            if i == 0:
                for c in weight_copies(n):
                    c.wait()
            active = jnp.maximum(dot(zd[:, :width], up[:, a:b], NN), 0.0)
            sq[:, a:b] = (active * active).astype(BF16)
            act_grad = dot(zd[:, width:], down[a:b, :], NT)
            hid[:, a:b] = (act_grad * 2.0 * active).astype(BF16)
            for c in result_copies(i, n):
                c.start()
            rows = dot(hid[:, a:b], up[:, a:b], NT)
            if n == 0:
                row_acc[...] = rows
            else:
                row_acc[...] += rows
        row_out[i * BLOCK : (i + 1) * BLOCK, :] = row_acc[...].astype(BF16)

    def drain(i):
        row_copy(i).wait()
        for n in range(len(chunks)):
            for c in result_copies(i, n):
                c.wait()

    def give_back(i):
        have = (lax.broadcasted_iota(jnp.int32, (total, BLOCK), 1) + i * BLOCK).astype(F32)
        put = jnp.where(jnp.broadcast_to(pos_col[:, 0:1], (total, BLOCK)) == have, 1.0, 0.0)
        return dot(put.astype(BF16), row_out[i * BLOCK : (i + 1) * BLOCK, :], NN)

    one_block(0)
    ret_ref[...] = give_back(0).astype(BF16)
    drain(0)

    @pl.when(count > BLOCK)
    def _():
        one_block(1)
        ret_ref[...] = (ret_ref[...].astype(F32) + give_back(1)).astype(BF16)
        drain(1)


def expert_pass(recv, up, down):
    total, twice = recv.shape
    width, units = up.shape
    n = len(chunks_of(units))
    vmem = pl.BlockSpec(memory_space=pltpu.VMEM)
    hbm = pl.BlockSpec(memory_space=pl.ANY)
    return pl.pallas_call(
        expert_kernel,
        in_specs=[vmem, hbm, hbm],
        out_specs=[vmem, hbm, hbm, hbm, pl.BlockSpec(memory_space=pltpu.SMEM)],
        out_shape=[
            jax.ShapeDtypeStruct((total, width), BF16),
            jax.ShapeDtypeStruct((total, twice), BF16),
            jax.ShapeDtypeStruct((total, units), BF16),
            jax.ShapeDtypeStruct((total, units), BF16),
            jax.ShapeDtypeStruct((1, 1), jnp.int32),
        ],
        scratch_shapes=[
            pltpu.VMEM((width, units), BF16),
            pltpu.VMEM((units, width), BF16),
            pltpu.VMEM((BLOCK, twice), BF16),
            pltpu.VMEM((BLOCK, units), BF16),
            pltpu.VMEM((BLOCK, units), BF16),
            pltpu.VMEM((BLOCK, width), F32),
            pltpu.VMEM((total, width), BF16),
            pltpu.VMEM((total, 128), F32),
            pltpu.VMEM((128, total), F32),
            pltpu.SemaphoreType.DMA((2 * n,)),
            pltpu.SemaphoreType.DMA((2 * n,)),
            pltpu.SemaphoreType.DMA,
        ],
        compiler_params=pltpu.CompilerParams(vmem_limit_bytes=VMEM_LIMIT),
        name="expert",
    )(recv, up, down)


def weight_kernel(count_ref, zd_ref, sq_ref, hid_ref, up_ref, down_ref):
    width = zd_ref.shape[1] // 2

    def emit(rows):
        down_ref[0] = dot(sq_ref[:rows, :], zd_ref[:rows, width:], TN).astype(BF16)
        up_ref[0] = dot(zd_ref[:rows, :width], hid_ref[:rows, :], TN).astype(BF16)

    @pl.when(count_ref[0, 0] <= BLOCK)
    def _():
        emit(BLOCK)

    @pl.when(count_ref[0, 0] > BLOCK)
    def _():
        emit(2 * BLOCK)


def weight_grads(count, zd, sq, hid):
    total, twice = zd.shape
    width, units = twice // 2, sq.shape[1]
    tile = 384
    return pl.pallas_call(
        weight_kernel,
        grid=(units // tile,),
        in_specs=[
            pl.BlockSpec(memory_space=pltpu.SMEM),
            pl.BlockSpec((total, twice), lambda j: (0, 0)),
            pl.BlockSpec((total, tile), lambda j: (0, j)),
            pl.BlockSpec((total, tile), lambda j: (0, j)),
        ],
        out_specs=[
            pl.BlockSpec((1, width, tile), lambda j: (0, 0, j)),
            pl.BlockSpec((1, tile, width), lambda j: (0, j, 0)),
        ],
        out_shape=[
            jax.ShapeDtypeStruct((1, width, units), BF16),
            jax.ShapeDtypeStruct((1, units, width), BF16),
        ],
        compiler_params=pltpu.CompilerParams(vmem_limit_bytes=VMEM_LIMIT),
        cost_estimate=pl.CostEstimate(
            flops=4 * BLOCK * width * units, transcendentals=0, bytes_accessed=8 * width * units
        ),
        name="weight_grads",
    )(count, zd, sq, hid)


def exchange(x, axes):
    return lax.all_to_all(x, axes, split_axis=0, concat_axis=0, tiled=True)


def on_device(
    latent_in, latent_grad, route_ids, gate_values, up_weight, down_weight, inputs, proj_weight
):
    n_wide = lax.axis_size("wide")
    n_narrow = lax.axis_size("narrow")
    experts = n_wide * n_narrow
    both = ("wide", "narrow")
    tokens, width = latent_in.shape
    send, place = pack(route_ids, gate_values, latent_in, latent_grad)
    recv = exchange(send.reshape(experts, SLOTS, 2 * width), both)
    rows, zd, sq, hid, count = expert_pass(
        recv.reshape(experts * SLOTS, 2 * width), up_weight[0], down_weight[0]
    )
    returned = exchange(rows.reshape(experts, SLOTS, width), both)
    grad_up, grad_down = weight_grads(count, zd, sq, hid)
    returned, grad_up, grad_down = lax.optimization_barrier((returned, grad_up, grad_down))
    token_grad = dot(place, returned.reshape(experts * SLOTS, width), NN).astype(BF16)
    copies = jnp.broadcast_to(token_grad[None], (n_narrow, tokens, width))
    piece = exchange(copies, "narrow").reshape(n_narrow * tokens, width)
    columns = width // n_wide
    parts = dot(inputs, piece, TN).astype(BF16)
    parts = parts.reshape(inputs.shape[1], n_wide, columns).transpose(1, 0, 2)
    parts = exchange(parts, "wide")
    grad_proj = jnp.sum(parts.astype(F32), axis=0)
    grad_inputs = dot(piece, proj_weight, NT).astype(BF16)
    return (grad_up, grad_down, grad_inputs, grad_proj)


def solution(mesh):
    placed = (
        P(("wide", "narrow"), None),
        P(("wide", "narrow"), None),
        P(("wide", "narrow"), None),
        P(("wide", "narrow"), None),
        P(("wide", "narrow"), None, None),
        P(("wide", "narrow"), None, None),
        P("wide", "narrow"),
        P("narrow", None),
    )
    return jax.shard_map(
        on_device,
        mesh=mesh,
        in_specs=placed,
        out_specs=(
            P(("wide", "narrow"), None, None),
            P(("wide", "narrow"), None, None),
            P("wide", "narrow"),
            P("narrow", "wide"),
        ),
        check_vma=False,
    )
```

```python
import functools

import jax
import jax.numpy as jnp
from jax import lax
from jax.experimental import pallas as pl
from jax.experimental.pallas import tpu as pltpu
from jax.sharding import PartitionSpec as P

BF16 = jnp.bfloat16
F32 = jnp.float32
SLOTS = 8
BLOCK = 512
PACK_STEPS = 4
VMEM_LIMIT = 56 * 1024 * 1024


def dot(a, b, dims, **kw):
    return lax.dot_general(a, b, (dims, ((), ())), preferred_element_type=F32, **kw)


NN = ((1,), (0,))
NT = ((1,), (1,))
TN = ((0,), (0,))


def pack_kernel(route_ref, gate_ref, z_ref, g_ref, send_hbm, place_ref, send, sem):
    tokens, top = route_ref.shape
    experts = 128
    total, twice = send.shape
    width = twice // 2
    routes = route_ref[...]
    gates = gate_ref[...]
    expert_of = lax.broadcasted_iota(jnp.int32, (tokens, experts), 1)
    hits = jnp.zeros((tokens, experts), F32)
    weights = jnp.zeros((tokens, experts), F32)
    for k in range(top):
        same = routes[:, k : k + 1] == expert_of
        hits = jnp.where(same, 1.0, hits)
        weights = jnp.where(same, gates[:, k : k + 1], weights)
    before = lax.broadcasted_iota(jnp.int32, (tokens, tokens), 1) < lax.broadcasted_iota(
        jnp.int32, (tokens, tokens), 0
    )
    rank = dot(before.astype(F32).astype(BF16), hits.astype(BF16), NN)
    rank = jnp.where(hits > 0, rank, -1.0).astype(BF16)
    rows = total // PACK_STEPS
    copies = []
    for p in range(PACK_STEPS):
        r = slice(p * rows, (p + 1) * rows)
        row = lax.broadcasted_iota(jnp.int32, (rows, experts), 0) + p * rows
        expert = lax.broadcasted_iota(jnp.int32, (rows, experts), 1)
        spread = jnp.where((row >> 3) == expert, 1.0, 0.0)
        spread_bf = spread.astype(BF16)
        slot = lax.broadcasted_iota(jnp.int32, (rows, tokens), 0) & (SLOTS - 1)
        chosen = jnp.where(dot(spread_bf, rank, NT) == slot.astype(F32), 1.0, 0.0)
        gate = jnp.sum(
            chosen * dot(spread, weights, NT, precision=lax.Precision.HIGHEST),
            axis=1,
            keepdims=True,
        )
        chosen = chosen.astype(BF16)
        send[r, :width] = dot(chosen, z_ref[...], NN).astype(BF16)
        send[r, width:] = (dot(chosen, g_ref[...], NN) * gate).astype(BF16)
        copies.append(pltpu.make_async_copy(send.at[r, :], send_hbm.at[r, :], sem.at[p]))
        copies[-1].start()
        slot_t = lax.broadcasted_iota(jnp.int32, (tokens, rows), 1) & (SLOTS - 1)
        place_ref[:, r] = jnp.where(
            dot(rank, spread_bf, NT) == slot_t.astype(F32), 1.0, 0.0
        ).astype(BF16)
    for c in copies:
        c.wait()


def pack(routes, gates, z, g):
    tokens, width = z.shape
    total = 128 * SLOTS
    vmem = pl.BlockSpec(memory_space=pltpu.VMEM)
    return pl.pallas_call(
        pack_kernel,
        in_specs=[vmem] * 4,
        out_specs=[pl.BlockSpec(memory_space=pl.ANY), vmem],
        out_shape=[
            jax.ShapeDtypeStruct((total, 2 * width), BF16),
            jax.ShapeDtypeStruct((tokens, total), BF16),
        ],
        scratch_shapes=[
            pltpu.VMEM((total, 2 * width), BF16),
            pltpu.SemaphoreType.DMA((PACK_STEPS,)),
        ],
        compiler_params=pltpu.CompilerParams(vmem_limit_bytes=VMEM_LIMIT),
        name="pack",
    )(routes, gates, z, g)


def chunks_of(hidden_units):
    sizes = (256, 768, 768, 512)
    edges = [0]
    for size in sizes:
        edges.append(edges[-1] + size)
    edges.append(hidden_units)
    return list(zip(edges[:-1], edges[1:]))


def expert_kernel(
    recv_hbm, up_hbm, down_hbm, ret_hbm, sq_hbm, hid_hbm,
    recv, up, down, sq, hid, row_acc, row_out, recv_sem, up_sem, down_sem, sq_sem, hid_sem, ret_sem,
):
    total, twice = recv.shape
    width = twice // 2
    chunks = chunks_of(up.shape[1])
    blocks = total // BLOCK

    def rows_of(i):
        return slice(i * BLOCK, (i + 1) * BLOCK)

    def copy_recv(i, half):
        at = (rows_of(i), slice(half * width, (half + 1) * width))
        return pltpu.make_async_copy(recv_hbm.at[at], recv.at[at], recv_sem.at[2 * i + half])

    def copy_up(n):
        at = (slice(None), slice(*chunks[n]))
        return pltpu.make_async_copy(up_hbm.at[at], up.at[at], up_sem.at[n])

    def copy_down(n):
        at = (slice(*chunks[n]), slice(None))
        return pltpu.make_async_copy(down_hbm.at[at], down.at[at], down_sem.at[n])

    def copy_out(i, n):
        at = (rows_of(i), slice(*chunks[n]))
        k = i * len(chunks) + n
        return (
            pltpu.make_async_copy(sq.at[at], sq_hbm.at[at], sq_sem.at[k]),
            pltpu.make_async_copy(hid.at[at], hid_hbm.at[at], hid_sem.at[k]),
        )

    def copy_ret(i):
        return pltpu.make_async_copy(row_out.at[rows_of(i)], ret_hbm.at[rows_of(i)], ret_sem.at[i])

    copy_up(0).start()
    copy_recv(0, 0).start()
    copy_down(0).start()
    copy_recv(0, 1).start()
    for n in range(1, len(chunks)):
        copy_up(n).start()
        copy_down(n).start()
    for i in range(1, blocks):
        copy_recv(i, 0).start()
        copy_recv(i, 1).start()
    for i in range(blocks):
        r = rows_of(i)
        copy_recv(i, 0).wait()
        for n, (a, b) in enumerate(chunks):
            if i == 0:
                copy_up(n).wait()
            active = jnp.maximum(dot(recv[r, :width], up[:, a:b], NN), 0.0)
            sq[r, a:b] = (active * active).astype(BF16)
            if n == 0:
                copy_recv(i, 1).wait()
            if i == 0:
                copy_down(n).wait()
            act_grad = dot(recv[r, width:], down[a:b, :], NT)
            hid[r, a:b] = (act_grad * 2.0 * active).astype(BF16)
            for c in copy_out(i, n):
                c.start()
            rows = dot(hid[r, a:b], up[:, a:b], NT)
            if n == 0:
                row_acc[...] = rows
            elif n < len(chunks) - 1:
                row_acc[...] += rows
            else:
                row_out[r, :] = (row_acc[...] + rows).astype(BF16)
        copy_ret(i).start()
    for i in range(blocks):
        for n in range(len(chunks)):
            for c in copy_out(i, n):
                c.wait()
        copy_ret(i).wait()


def expert_pass(recv, up, down):
    total, twice = recv.shape
    width, units = up.shape
    n = len(chunks_of(units))
    blocks = total // BLOCK
    hbm = pl.BlockSpec(memory_space=pl.ANY)
    dma = pltpu.SemaphoreType.DMA
    return pl.pallas_call(
        expert_kernel,
        in_specs=[hbm] * 3,
        out_specs=[hbm] * 3,
        out_shape=[
            jax.ShapeDtypeStruct((total, width), BF16),
            jax.ShapeDtypeStruct((total, units), BF16),
            jax.ShapeDtypeStruct((total, units), BF16),
        ],
        scratch_shapes=[
            pltpu.VMEM((total, twice), BF16),
            pltpu.VMEM((width, units), BF16),
            pltpu.VMEM((units, width), BF16),
            pltpu.VMEM((total, units), BF16),
            pltpu.VMEM((total, units), BF16),
            pltpu.VMEM((BLOCK, width), F32),
            pltpu.VMEM((total, width), BF16),
            dma((2 * blocks,)),
            dma((n,)),
            dma((n,)),
            dma((blocks * n,)),
            dma((blocks * n,)),
            dma((blocks,)),
        ],
        compiler_params=pltpu.CompilerParams(vmem_limit_bytes=VMEM_LIMIT),
        name="expert",
    )(recv, up, down)


def weight_kernel(zd_ref, sq_ref, hid_ref, up_ref, down_ref):
    width = zd_ref.shape[1] // 2
    down_ref[0] = dot(sq_ref[...], zd_ref[:, width:], TN).astype(BF16)
    up_ref[0] = dot(zd_ref[:, :width], hid_ref[...], TN).astype(BF16)


def weight_grads(zd, sq, hid):
    total, twice = zd.shape
    width, units = twice // 2, sq.shape[1]
    tile = 384
    return pl.pallas_call(
        weight_kernel,
        grid=(units // tile,),
        in_specs=[
            pl.BlockSpec((total, twice), lambda j: (0, 0)),
            pl.BlockSpec((total, tile), lambda j: (0, j)),
            pl.BlockSpec((total, tile), lambda j: (0, j)),
        ],
        out_specs=[
            pl.BlockSpec((1, width, tile), lambda j: (0, 0, j)),
            pl.BlockSpec((1, tile, width), lambda j: (0, j, 0)),
        ],
        out_shape=[
            jax.ShapeDtypeStruct((1, width, units), BF16),
            jax.ShapeDtypeStruct((1, units, width), BF16),
        ],
        compiler_params=pltpu.CompilerParams(vmem_limit_bytes=VMEM_LIMIT),
        cost_estimate=pl.CostEstimate(
            flops=4 * total * width * units, transcendentals=0, bytes_accessed=8 * width * units
        ),
        name="weight_grads",
    )(zd, sq, hid)


def part_kernel(inputs_ref, piece_ref, parts_ref):
    n_parts, _, columns = parts_ref.shape
    acc = dot(inputs_ref[...], piece_ref[...], TN)
    for p in range(n_parts):
        parts_ref[p] = acc[:, p * columns : (p + 1) * columns].astype(BF16)


def proj_parts(inputs, piece, n_parts):
    vmem = pl.BlockSpec(memory_space=pltpu.VMEM)
    return pl.pallas_call(
        part_kernel,
        in_specs=[vmem, vmem],
        out_specs=vmem,
        out_shape=jax.ShapeDtypeStruct(
            (n_parts, inputs.shape[1], piece.shape[1] // n_parts), BF16
        ),
        name="proj_parts",
    )(inputs, piece)


def exchange(x, axes):
    return lax.all_to_all(x, axes, split_axis=0, concat_axis=0, tiled=True)


def on_device(
    latent_in, latent_grad, route_ids, gate_values, up_weight, down_weight, inputs, proj_weight
):
    n_wide = lax.axis_size("wide")
    n_narrow = lax.axis_size("narrow")
    experts = n_wide * n_narrow
    both = ("wide", "narrow")
    tokens, width = latent_in.shape
    send, place = pack(route_ids, gate_values, latent_in, latent_grad)
    recv = exchange(send.reshape(experts, SLOTS, 2 * width), both)
    recv = recv.reshape(experts * SLOTS, 2 * width)
    rows, sq, hid = expert_pass(recv, up_weight[0], down_weight[0])
    returned = exchange(rows.reshape(experts, SLOTS, width), both)
    grad_up, grad_down = weight_grads(recv, sq, hid)
    returned, grad_up, grad_down = lax.optimization_barrier((returned, grad_up, grad_down))
    token_grad = dot(place, returned.reshape(experts * SLOTS, width), NN).astype(BF16)
    copies = jnp.broadcast_to(token_grad[None], (n_narrow, tokens, width))
    piece = exchange(copies, "narrow").reshape(n_narrow * tokens, width)
    parts = exchange(proj_parts(inputs, piece, n_wide), "wide")
    grad_proj = jnp.sum(parts.astype(F32), axis=0)
    grad_inputs = dot(piece, proj_weight, NT).astype(BF16)
    return (grad_up, grad_down, grad_inputs, grad_proj)


def solution(mesh):
    placed = (
        P(("wide", "narrow"), None),
        P(("wide", "narrow"), None),
        P(("wide", "narrow"), None),
        P(("wide", "narrow"), None),
        P(("wide", "narrow"), None, None),
        P(("wide", "narrow"), None, None),
        P("wide", "narrow"),
        P("narrow", None),
    )
    return jax.shard_map(
        on_device,
        mesh=mesh,
        in_specs=placed,
        out_specs=(
            P(("wide", "narrow"), None, None),
            P(("wide", "narrow"), None, None),
            P("wide", "narrow"),
            P("narrow", "wide"),
        ),
        check_vma=False,
    )
```

```python
import functools

import jax
import jax.numpy as jnp
from jax import lax
from jax.experimental import pallas as pl
from jax.experimental.pallas import tpu as pltpu
from jax.sharding import PartitionSpec as P

BF16 = jnp.bfloat16
F32 = jnp.float32
SLOTS = 8
BLOCK = 512
CHUNK = 768
PACK_STEPS = 4
VMEM_LIMIT = 28 * 1024 * 1024


def dot(a, b, dims, **kw):
    return lax.dot_general(a, b, (dims, ((), ())), preferred_element_type=F32, **kw)


NN = ((1,), (0,))
NT = ((1,), (1,))
TN = ((0,), (0,))


def pack_kernel(
    route_hbm, gate_hbm, z_hbm, g_hbm, send, place_ref, route_ref, gate_ref, z_ref, g_ref, sem
):
    pairs = ((route_hbm, route_ref), (gate_hbm, gate_ref), (z_hbm, z_ref), (g_hbm, g_ref))
    loads = [pltpu.make_async_copy(a, b, sem.at[i]) for i, (a, b) in enumerate(pairs)]
    for c in loads:
        c.start()
    tokens, top = route_ref.shape
    experts = 128
    total, twice = send.shape
    width = twice // 2
    for c in loads:
        c.wait()
    routes = route_ref[...]
    gates = gate_ref[...]
    expert_of = lax.broadcasted_iota(jnp.int32, (tokens, experts), 1)
    hits = jnp.zeros((tokens, experts), F32)
    weights = jnp.zeros((tokens, experts), F32)
    for k in range(top):
        same = routes[:, k : k + 1] == expert_of
        hits = jnp.where(same, 1.0, hits)
        weights = jnp.where(same, gates[:, k : k + 1], weights)
    before = lax.broadcasted_iota(jnp.int32, (tokens, tokens), 1) < lax.broadcasted_iota(
        jnp.int32, (tokens, tokens), 0
    )
    rank = dot(before.astype(F32).astype(BF16), hits.astype(BF16), NN)
    rank = jnp.where(hits > 0, rank, -1.0).astype(BF16)
    rows = total // PACK_STEPS
    for p in range(PACK_STEPS):
        r = slice(p * rows, (p + 1) * rows)
        row = lax.broadcasted_iota(jnp.int32, (rows, experts), 0) + p * rows
        expert = lax.broadcasted_iota(jnp.int32, (rows, experts), 1)
        spread = jnp.where((row >> 3) == expert, 1.0, 0.0)
        spread_bf = spread.astype(BF16)
        slot = lax.broadcasted_iota(jnp.int32, (rows, tokens), 0) & (SLOTS - 1)
        chosen = jnp.where(dot(spread_bf, rank, NT) == slot.astype(F32), 1.0, 0.0)
        gate = jnp.sum(
            chosen * dot(spread, weights, NT, precision=lax.Precision.HIGHEST),
            axis=1,
            keepdims=True,
        )
        chosen = chosen.astype(BF16)
        send[r, :width] = dot(chosen, z_ref[...], NN).astype(BF16)
        send[r, width:] = (dot(chosen, g_ref[...], NN) * gate).astype(BF16)
        slot_t = lax.broadcasted_iota(jnp.int32, (tokens, rows), 1) & (SLOTS - 1)
        place_ref[:, r] = jnp.where(
            dot(rank, spread_bf, NT) == slot_t.astype(F32), 1.0, 0.0
        ).astype(BF16)


def pack(routes, gates, z, g):
    tokens, width = z.shape
    total = 128 * SLOTS
    vmem = pl.BlockSpec(memory_space=pltpu.VMEM)
    return pl.pallas_call(
        pack_kernel,
        in_specs=[pl.BlockSpec(memory_space=pltpu.HBM)] * 4,
        out_specs=[vmem, vmem],
        out_shape=[pltpu.VMEM((total, 2 * width), BF16), pltpu.VMEM((tokens, total), BF16)],
        scratch_shapes=[pltpu.VMEM(x.shape, x.dtype) for x in (routes, gates, z, g)]
        + [pltpu.SemaphoreType.DMA((4,))],
        compiler_params=pltpu.CompilerParams(vmem_limit_bytes=VMEM_LIMIT),
        name="pack",
    )(*(pltpu.with_memory_space_constraint(x, pltpu.HBM) for x in (routes, gates, z, g)))


def expert_kernel(
    recv, up, down_hbm, ret_hbm, sq_hbm, hid_hbm,
    down, ret, sq, hid, down_sem, ret_sem, sq_sem, hid_sem,
):
    total, twice = recv.shape
    width = twice // 2
    edges = [*range(0, up.shape[1], CHUNK), up.shape[1]]
    spans = [slice(a, b) for a, b in zip(edges[:-1], edges[1:])]
    weights = [
        pltpu.make_async_copy(down_hbm.at[c, :], down.at[c, :], down_sem.at[n])
        for n, c in enumerate(spans)
    ]
    for w in weights:
        w.start()
    outs = []

    def send_out(src, dst, sem, at):
        outs.append(pltpu.make_async_copy(src.at[at], dst.at[at], sem))
        outs[-1].start()

    for i in range(total // BLOCK):
        r = slice(i * BLOCK, (i + 1) * BLOCK)
        for n, c in enumerate(spans):
            active = jnp.maximum(dot(recv[r, :width], up[:, c], NN), 0.0)
            sq[r, c] = (active * active).astype(BF16)
            if i == 0:
                weights[n].wait()
            act_grad = dot(recv[r, width:], down[c, :], NT)
            hid[r, c] = (act_grad * 2.0 * active).astype(BF16)
            k = i * len(spans) + n
            send_out(sq, sq_hbm, sq_sem.at[k], (r, c))
            send_out(hid, hid_hbm, hid_sem.at[k], (r, c))
        for h in range(2):
            q = slice(i * BLOCK + h * BLOCK // 2, i * BLOCK + (h + 1) * BLOCK // 2)
            ret[q, :] = dot(hid[q, :], up[...], NT).astype(BF16)
            send_out(ret, ret_hbm, ret_sem.at[2 * i + h], (q, slice(None)))
    for c in outs:
        c.wait()


def on_chip(x):
    return pltpu.with_memory_space_constraint(x, pltpu.VMEM)


def expert_pass(recv, up, down):
    total, twice = recv.shape
    width, units = up.shape
    vmem = pl.BlockSpec(memory_space=pltpu.VMEM)
    hbm = pl.BlockSpec(memory_space=pltpu.HBM)
    spans = -(-units // CHUNK)
    blocks = total // BLOCK
    dma = pltpu.SemaphoreType.DMA
    return pl.pallas_call(
        expert_kernel,
        in_specs=[vmem, vmem, hbm],
        out_specs=[hbm] * 3,
        out_shape=[
            pltpu.HBM((total, width), BF16),
            pltpu.HBM((total, units), BF16),
            pltpu.HBM((total, units), BF16),
        ],
        scratch_shapes=[
            pltpu.VMEM((units, width), BF16),
            pltpu.VMEM((total, width), BF16),
            pltpu.VMEM((total, units), BF16),
            pltpu.VMEM((total, units), BF16),
            dma((spans,)),
            dma((2 * blocks,)),
            dma((blocks * spans,)),
            dma((blocks * spans,)),
        ],
        compiler_params=pltpu.CompilerParams(vmem_limit_bytes=VMEM_LIMIT),
        name="expert",
    )(on_chip(recv), on_chip(up), pltpu.with_memory_space_constraint(down, pltpu.HBM))


def weight_kernel(zd_ref, sq_ref, hid_ref, up_ref, down_ref):
    width = zd_ref.shape[1] // 2
    down_ref[0] = dot(sq_ref[...], zd_ref[:, width:], TN).astype(BF16)
    up_ref[0] = dot(zd_ref[:, :width], hid_ref[...], TN).astype(BF16)


def weight_grads(zd, sq, hid):
    total, twice = zd.shape
    width, units = twice // 2, sq.shape[1]
    tile = 384
    return pl.pallas_call(
        weight_kernel,
        grid=(units // tile,),
        in_specs=[
            pl.BlockSpec((total, twice), lambda j: (0, 0)),
            pl.BlockSpec((total, tile), lambda j: (0, j)),
            pl.BlockSpec((total, tile), lambda j: (0, j)),
        ],
        out_specs=[
            pl.BlockSpec((1, width, tile), lambda j: (0, 0, j)),
            pl.BlockSpec((1, tile, width), lambda j: (0, j, 0)),
        ],
        out_shape=[
            jax.ShapeDtypeStruct((1, width, units), BF16),
            jax.ShapeDtypeStruct((1, units, width), BF16),
        ],
        compiler_params=pltpu.CompilerParams(vmem_limit_bytes=2 * VMEM_LIMIT),
        cost_estimate=pl.CostEstimate(
            flops=4 * total * width * units, transcendentals=0, bytes_accessed=8 * width * units
        ),
        name="weight_grads",
    )(zd, sq, hid)


def part_kernel(inputs_ref, piece_ref, parts_ref):
    n_parts, _, columns = parts_ref.shape
    acc = dot(inputs_ref[...], piece_ref[...], TN)
    for p in range(n_parts):
        parts_ref[p] = acc[:, p * columns : (p + 1) * columns].astype(BF16)


def proj_parts(inputs, piece, n_parts):
    vmem = pl.BlockSpec(memory_space=pltpu.VMEM)
    return pl.pallas_call(
        part_kernel,
        in_specs=[vmem, vmem],
        out_specs=vmem,
        out_shape=jax.ShapeDtypeStruct(
            (n_parts, inputs.shape[1], piece.shape[1] // n_parts), BF16
        ),
        compiler_params=pltpu.CompilerParams(vmem_limit_bytes=VMEM_LIMIT),
        name="proj_parts",
    )(on_chip(inputs), on_chip(piece))


def exchange(x, axes):
    return lax.all_to_all(x, axes, split_axis=0, concat_axis=0, tiled=True)


def on_device(
    latent_in, latent_grad, route_ids, gate_values, up_weight, down_weight, inputs, proj_weight
):
    n_wide = lax.axis_size("wide")
    n_narrow = lax.axis_size("narrow")
    experts = n_wide * n_narrow
    both = ("wide", "narrow")
    tokens, width = latent_in.shape
    send, place = pack(route_ids, gate_values, latent_in, latent_grad)
    recv = exchange(send.reshape(experts, SLOTS, 2 * width), both)
    recv = recv.reshape(experts * SLOTS, 2 * width)
    rows, sq, hid = expert_pass(recv, up_weight[0], down_weight[0])
    returned = exchange(rows.reshape(experts, SLOTS, width), both)
    grad_up, grad_down = weight_grads(recv, sq, hid)
    returned, grad_up, grad_down = lax.optimization_barrier((returned, grad_up, grad_down))
    token_grad = dot(place, returned.reshape(experts * SLOTS, width), NN).astype(BF16)
    copies = jnp.broadcast_to(token_grad[None], (n_narrow, tokens, width))
    piece = exchange(copies, "narrow").reshape(n_narrow * tokens, width)
    parts = exchange(proj_parts(inputs, piece, n_wide), "wide")
    grad_proj = jnp.sum(parts.astype(F32), axis=0)
    grad_inputs = dot(piece, proj_weight, NT).astype(BF16)
    return (grad_up, grad_down, grad_inputs, grad_proj)


def solution(mesh):
    placed = (
        P(("wide", "narrow"), None),
        P(("wide", "narrow"), None),
        P(("wide", "narrow"), None),
        P(("wide", "narrow"), None),
        P(("wide", "narrow"), None, None),
        P(("wide", "narrow"), None, None),
        P("wide", "narrow"),
        P("narrow", None),
    )
    return jax.shard_map(
        on_device,
        mesh=mesh,
        in_specs=placed,
        out_specs=(
            P(("wide", "narrow"), None, None),
            P(("wide", "narrow"), None, None),
            P("wide", "narrow"),
            P("narrow", "wide"),
        ),
        check_vma=False,
    )
```

```python
import functools

import jax
import jax.numpy as jnp
from jax import lax
from jax.experimental import pallas as pl
from jax.experimental.pallas import tpu as pltpu
from jax.sharding import PartitionSpec as P

BF16 = jnp.bfloat16
F32 = jnp.float32
SLOTS = 8
BLOCK = 512
CHUNK = 768
PACK_STEPS = 4
VMEM_LIMIT = 28 * 1024 * 1024


def dot(a, b, dims, **kw):
    return lax.dot_general(a, b, (dims, ((), ())), preferred_element_type=F32, **kw)


NN = ((1,), (0,))
NT = ((1,), (1,))
TN = ((0,), (0,))


def pack_kernel(
    route_hbm, gate_hbm, z_hbm, g_hbm, down_hbm,
    send, place_ref, down, route_ref, gate_ref, z_ref, g_ref, sem,
):
    pairs = ((route_hbm, route_ref), (gate_hbm, gate_ref), (z_hbm, z_ref), (g_hbm, g_ref))
    loads = [pltpu.make_async_copy(a, b, sem.at[i]) for i, (a, b) in enumerate(pairs)]
    for c in loads:
        c.start()
    fetch_down = pltpu.make_async_copy(down_hbm, down, sem.at[len(loads)])
    fetch_down.start()
    tokens, top = route_ref.shape
    experts = 128
    total, twice = send.shape
    width = twice // 2
    for c in loads:
        c.wait()
    routes = route_ref[...]
    gates = gate_ref[...]
    expert_of = lax.broadcasted_iota(jnp.int32, (tokens, experts), 1)
    hits = jnp.zeros((tokens, experts), F32)
    weights = jnp.zeros((tokens, experts), F32)
    for k in range(top):
        same = routes[:, k : k + 1] == expert_of
        hits = jnp.where(same, 1.0, hits)
        weights = jnp.where(same, gates[:, k : k + 1], weights)
    before = lax.broadcasted_iota(jnp.int32, (tokens, tokens), 1) < lax.broadcasted_iota(
        jnp.int32, (tokens, tokens), 0
    )
    rank = dot(before.astype(F32).astype(BF16), hits.astype(BF16), NN)
    rank = jnp.where(hits > 0, rank, -1.0).astype(BF16)
    rows = total // PACK_STEPS
    for p in range(PACK_STEPS):
        r = slice(p * rows, (p + 1) * rows)
        row = lax.broadcasted_iota(jnp.int32, (rows, experts), 0) + p * rows
        expert = lax.broadcasted_iota(jnp.int32, (rows, experts), 1)
        spread = jnp.where((row >> 3) == expert, 1.0, 0.0)
        spread_bf = spread.astype(BF16)
        slot = lax.broadcasted_iota(jnp.int32, (rows, tokens), 0) & (SLOTS - 1)
        chosen = jnp.where(dot(spread_bf, rank, NT) == slot.astype(F32), 1.0, 0.0)
        gate = jnp.sum(
            chosen * dot(spread, weights, NT, precision=lax.Precision.HIGHEST),
            axis=1,
            keepdims=True,
        )
        chosen = chosen.astype(BF16)
        send[r, :width] = dot(chosen, z_ref[...], NN).astype(BF16)
        send[r, width:] = (dot(chosen, g_ref[...], NN) * gate).astype(BF16)
        slot_t = lax.broadcasted_iota(jnp.int32, (tokens, rows), 1) & (SLOTS - 1)
        place_ref[:, r] = jnp.where(
            dot(rank, spread_bf, NT) == slot_t.astype(F32), 1.0, 0.0
        ).astype(BF16)
    fetch_down.wait()


def in_hbm(x):
    return pltpu.with_memory_space_constraint(x, pltpu.HBM)


def pack(routes, gates, z, g, down):
    tokens, width = z.shape
    total = 128 * SLOTS
    vmem = pl.BlockSpec(memory_space=pltpu.VMEM)
    return pl.pallas_call(
        pack_kernel,
        in_specs=[pl.BlockSpec(memory_space=pltpu.HBM)] * 5,
        out_specs=[vmem] * 3,
        out_shape=[
            pltpu.VMEM((total, 2 * width), BF16),
            pltpu.VMEM((tokens, total), BF16),
            pltpu.VMEM(down.shape, BF16),
        ],
        scratch_shapes=[pltpu.VMEM(x.shape, x.dtype) for x in (routes, gates, z, g)]
        + [pltpu.SemaphoreType.DMA((5,))],
        compiler_params=pltpu.CompilerParams(vmem_limit_bytes=VMEM_LIMIT),
        name="pack",
    )(*(in_hbm(x) for x in (routes, gates, z, g, down)))


def expert_kernel(
    recv, up, down, ret_hbm, sq_hbm, hid_hbm,
    ret, sq, hid, ret_sem, sq_sem, hid_sem,
):
    total, twice = recv.shape
    width = twice // 2
    edges = [*range(0, up.shape[1], CHUNK), up.shape[1]]
    spans = [slice(a, b) for a, b in zip(edges[:-1], edges[1:])]
    outs = []

    def send_out(src, dst, sem, at):
        outs.append(pltpu.make_async_copy(src.at[at], dst.at[at], sem))
        outs[-1].start()

    for i in range(total // BLOCK):
        r = slice(i * BLOCK, (i + 1) * BLOCK)
        for n, c in enumerate(spans):
            active = jnp.maximum(dot(recv[r, :width], up[:, c], NN), 0.0)
            sq[r, c] = (active * active).astype(BF16)
            act_grad = dot(recv[r, width:], down[c, :], NT)
            hid[r, c] = (act_grad * 2.0 * active).astype(BF16)
            k = i * len(spans) + n
            send_out(sq, sq_hbm, sq_sem.at[k], (r, c))
            send_out(hid, hid_hbm, hid_sem.at[k], (r, c))
        for h in range(2):
            q = slice(i * BLOCK + h * BLOCK // 2, i * BLOCK + (h + 1) * BLOCK // 2)
            ret[q, :] = dot(hid[q, :], up[...], NT).astype(BF16)
            send_out(ret, ret_hbm, ret_sem.at[2 * i + h], (q, slice(None)))
    for c in outs:
        c.wait()


def on_chip(x):
    return pltpu.with_memory_space_constraint(x, pltpu.VMEM)


def expert_pass(recv, up, down):
    total, twice = recv.shape
    width, units = up.shape
    vmem = pl.BlockSpec(memory_space=pltpu.VMEM)
    hbm = pl.BlockSpec(memory_space=pltpu.HBM)
    spans = -(-units // CHUNK)
    blocks = total // BLOCK
    dma = pltpu.SemaphoreType.DMA
    return pl.pallas_call(
        expert_kernel,
        in_specs=[vmem] * 3,
        out_specs=[hbm] * 3,
        out_shape=[
            pltpu.HBM((total, width), BF16),
            pltpu.HBM((total, units), BF16),
            pltpu.HBM((total, units), BF16),
        ],
        scratch_shapes=[
            pltpu.VMEM((total, width), BF16),
            pltpu.VMEM((total, units), BF16),
            pltpu.VMEM((total, units), BF16),
            dma((2 * blocks,)),
            dma((blocks * spans,)),
            dma((blocks * spans,)),
        ],
        compiler_params=pltpu.CompilerParams(vmem_limit_bytes=VMEM_LIMIT),
        name="expert",
    )(on_chip(recv), on_chip(up), on_chip(down))


def weight_kernel(zd_ref, sq_ref, hid_ref, up_ref, down_ref):
    width = zd_ref.shape[1] // 2
    down_ref[0] = dot(sq_ref[...], zd_ref[:, width:], TN).astype(BF16)
    up_ref[0] = dot(zd_ref[:, :width], hid_ref[...], TN).astype(BF16)


def weight_grads(zd, sq, hid):
    total, twice = zd.shape
    width, units = twice // 2, sq.shape[1]
    tile = 384
    return pl.pallas_call(
        weight_kernel,
        grid=(units // tile,),
        in_specs=[
            pl.BlockSpec((total, twice), lambda j: (0, 0)),
            pl.BlockSpec((total, tile), lambda j: (0, j)),
            pl.BlockSpec((total, tile), lambda j: (0, j)),
        ],
        out_specs=[
            pl.BlockSpec((1, width, tile), lambda j: (0, 0, j)),
            pl.BlockSpec((1, tile, width), lambda j: (0, j, 0)),
        ],
        out_shape=[
            jax.ShapeDtypeStruct((1, width, units), BF16),
            jax.ShapeDtypeStruct((1, units, width), BF16),
        ],
        compiler_params=pltpu.CompilerParams(vmem_limit_bytes=2 * VMEM_LIMIT),
        cost_estimate=pl.CostEstimate(
            flops=4 * total * width * units, transcendentals=0, bytes_accessed=8 * width * units
        ),
        name="weight_grads",
    )(zd, sq, hid)


def share_kernel(spot_ref, inputs_ref, piece_ref, keep_ref, give_ref):
    pairs, _, columns = keep_ref.shape
    acc = dot(inputs_ref[...], piece_ref[...], TN)
    core = spot_ref[0] & 1

    def emit(mine):
        for p in range(pairs):
            for half in range(2):
                at = (2 * p + half) * columns
                part = acc[:, at : at + columns]
                if half == mine:
                    keep_ref[p] = part
                else:
                    give_ref[p] = part.astype(BF16)

    @pl.when(core == 0)
    def _():
        emit(0)

    @pl.when(core == 1)
    def _():
        emit(1)


def add_kernel(spot_ref, keep_ref, got_ref, *out_refs):
    pairs = keep_ref.shape[0]
    for d, out in enumerate(out_refs):
        p = lax.rem((spot_ref[0] >> 1) + d, pairs)
        out[...] = (keep_ref[p] + got_ref[p].astype(F32)).astype(out.dtype)


def reduce_over_wide(spot, inputs, piece, n_wide):
    rows, columns = inputs.shape[1], piece.shape[1] // n_wide
    pairs = n_wide // 2
    vmem = pl.BlockSpec(memory_space=pltpu.VMEM)
    smem = pl.BlockSpec(memory_space=pltpu.SMEM)
    params = pltpu.CompilerParams(vmem_limit_bytes=VMEM_LIMIT)
    keep, give = pl.pallas_call(
        share_kernel,
        in_specs=[smem, vmem, vmem],
        out_specs=[vmem, vmem],
        out_shape=[
            pltpu.VMEM((pairs, rows, columns), F32),
            jax.ShapeDtypeStruct((pairs, rows, columns), BF16),
        ],
        compiler_params=params,
        name="share",
    )(spot, on_chip(inputs), on_chip(piece))
    got = lax.ppermute(give, "wide", [(w, w ^ 1) for w in range(n_wide)])
    own, *others = pl.pallas_call(
        add_kernel,
        in_specs=[smem, vmem, vmem],
        out_specs=[vmem] * pairs,
        out_shape=[jax.ShapeDtypeStruct((rows, columns), F32)]
        + [jax.ShapeDtypeStruct((rows, columns), BF16)] * (pairs - 1),
        compiler_params=params,
        name="add",
    )(spot, on_chip(keep), on_chip(got))
    for d, part in enumerate(others, 1):
        line = [(w, ((w >> 1) + d) % pairs * 2 + (w & 1)) for w in range(n_wide)]
        own = own + lax.ppermute(part, "wide", line).astype(F32)
    return own


def exchange(x, axes):
    return lax.all_to_all(x, axes, split_axis=0, concat_axis=0, tiled=True)


def on_device(
    latent_in, latent_grad, route_ids, gate_values, up_weight, down_weight, inputs, proj_weight
):
    n_wide = lax.axis_size("wide")
    n_narrow = lax.axis_size("narrow")
    experts = n_wide * n_narrow
    both = ("wide", "narrow")
    tokens, width = latent_in.shape
    send, place, down = pack(route_ids, gate_values, latent_in, latent_grad, down_weight[0])
    recv = exchange(send.reshape(experts, SLOTS, 2 * width), both)
    recv = recv.reshape(experts * SLOTS, 2 * width)
    rows, sq, hid = expert_pass(recv, up_weight[0], down)
    returned = exchange(rows.reshape(experts, SLOTS, width), both)
    grad_up, grad_down = weight_grads(recv, sq, hid)
    spot = lax.axis_index("wide").astype(jnp.int32).reshape(1)
    returned, grad_up, grad_down, spot = lax.optimization_barrier(
        (returned, grad_up, grad_down, spot)
    )
    token_grad = dot(place, returned.reshape(experts * SLOTS, width), NN).astype(BF16)
    copies = jnp.broadcast_to(token_grad[None], (n_narrow, tokens, width))
    piece = exchange(copies, "narrow").reshape(n_narrow * tokens, width)
    grad_proj = reduce_over_wide(spot, inputs, piece, n_wide)
    grad_inputs = dot(piece, proj_weight, NT).astype(BF16)
    return (grad_up, grad_down, grad_inputs, grad_proj)


def solution(mesh):
    placed = (
        P(("wide", "narrow"), None),
        P(("wide", "narrow"), None),
        P(("wide", "narrow"), None),
        P(("wide", "narrow"), None),
        P(("wide", "narrow"), None, None),
        P(("wide", "narrow"), None, None),
        P("wide", "narrow"),
        P("narrow", None),
    )
    return jax.shard_map(
        on_device,
        mesh=mesh,
        in_specs=placed,
        out_specs=(
            P(("wide", "narrow"), None, None),
            P(("wide", "narrow"), None, None),
            P("wide", "narrow"),
            P("narrow", "wide"),
        ),
        check_vma=False,
    )
```

```python
import functools

import jax
import jax.numpy as jnp
from jax import lax
from jax.experimental import pallas as pl
from jax.experimental.pallas import tpu as pltpu
from jax.sharding import PartitionSpec as P

BF16 = jnp.bfloat16
F32 = jnp.float32
SLOTS = 8
BLOCK = 512
CHUNK = 768
PACK_STEPS = 2
VMEM_LIMIT = 28 * 1024 * 1024


def dot(a, b, dims):
    return lax.dot_general(a, b, (dims, ((), ())), preferred_element_type=F32)


NN = ((1,), (0,))
NT = ((1,), (1,))
TN = ((0,), (0,))


def pack_kernel(
    route_hbm, gate_hbm, z_hbm, g_hbm, down_hbm,
    send, place_ref, down, route_ref, gate_ref, z_ref, g_ref, sem,
):
    pairs = ((route_hbm, route_ref), (gate_hbm, gate_ref), (z_hbm, z_ref), (g_hbm, g_ref))
    loads = [pltpu.make_async_copy(a, b, sem.at[i]) for i, (a, b) in enumerate(pairs)]
    for c in loads:
        c.start()
    fetch_down = pltpu.make_async_copy(down_hbm, down, sem.at[len(loads)])
    fetch_down.start()
    tokens, top = route_ref.shape
    experts = 128
    total, twice = send.shape
    width = twice // 2
    for c in loads:
        c.wait()
    routes = route_ref[...]
    gates = gate_ref[...]
    expert_of = lax.broadcasted_iota(jnp.int32, (tokens, experts), 1)
    hits = jnp.zeros((tokens, experts), F32)
    weights = jnp.zeros((tokens, experts), F32)
    for k in range(top):
        same = routes[:, k : k + 1] == expert_of
        hits = jnp.where(same, 1.0, hits)
        weights = jnp.where(same, gates[:, k : k + 1], weights)
    before = lax.broadcasted_iota(jnp.int32, (tokens, tokens), 1) < lax.broadcasted_iota(
        jnp.int32, (tokens, tokens), 0
    )
    rank = dot(before.astype(F32).astype(BF16), hits.astype(BF16), NN)
    rank = jnp.where(hits > 0, rank, -1.0).astype(BF16)
    terms = []
    for _ in range(3):
        terms.append(weights.astype(BF16))
        weights = weights - terms[-1].astype(F32)
    rows = total // PACK_STEPS
    for p in range(PACK_STEPS):
        r = slice(p * rows, (p + 1) * rows)
        row = lax.broadcasted_iota(jnp.int32, (rows, experts), 0) + p * rows
        expert = lax.broadcasted_iota(jnp.int32, (rows, experts), 1)
        spread_bf = jnp.where((row >> 3) == expert, 1.0, 0.0).astype(BF16)
        slot = lax.broadcasted_iota(jnp.int32, (rows, tokens), 0) & (SLOTS - 1)
        chosen = jnp.where(dot(spread_bf, rank, NT) == slot.astype(F32), 1.0, 0.0)
        gate = sum(dot(spread_bf, term, NT) for term in terms)
        gate = jnp.sum(chosen * gate, axis=1, keepdims=True)
        chosen = chosen.astype(BF16)
        send[r, :width] = dot(chosen, z_ref[...], NN).astype(BF16)
        send[r, width:] = (dot(chosen, g_ref[...], NN) * gate).astype(BF16)
        slot_t = lax.broadcasted_iota(jnp.int32, (tokens, rows), 1) & (SLOTS - 1)
        place_ref[:, r] = jnp.where(
            dot(rank, spread_bf, NT) == slot_t.astype(F32), 1.0, 0.0
        ).astype(BF16)
    fetch_down.wait()


def in_hbm(x):
    return pltpu.with_memory_space_constraint(x, pltpu.HBM)


def pack(routes, gates, z, g, down):
    tokens, width = z.shape
    total = 128 * SLOTS
    vmem = pl.BlockSpec(memory_space=pltpu.VMEM)
    return pl.pallas_call(
        pack_kernel,
        in_specs=[pl.BlockSpec(memory_space=pltpu.HBM)] * 5,
        out_specs=[vmem] * 3,
        out_shape=[
            pltpu.VMEM((total, 2 * width), BF16),
            pltpu.VMEM((tokens, total), BF16),
            pltpu.VMEM(down.shape, BF16),
        ],
        scratch_shapes=[pltpu.VMEM(x.shape, x.dtype) for x in (routes, gates, z, g)]
        + [pltpu.SemaphoreType.DMA((5,))],
        compiler_params=pltpu.CompilerParams(vmem_limit_bytes=VMEM_LIMIT),
        name="pack",
    )(*(in_hbm(x) for x in (routes, gates, z, g, down)))


def expert_kernel(
    recv, up, down, ret_hbm, sq_hbm, hid_hbm,
    ret, sq, hid, ret_sem, sq_sem, hid_sem,
):
    total, twice = recv.shape
    width = twice // 2
    edges = [*range(0, up.shape[1], CHUNK), up.shape[1]]
    spans = [slice(a, b) for a, b in zip(edges[:-1], edges[1:])]
    outs = []

    def send_out(src, dst, sem, at):
        outs.append(pltpu.make_async_copy(src.at[at], dst.at[at], sem))
        outs[-1].start()

    for i in range(total // BLOCK):
        r = slice(i * BLOCK, (i + 1) * BLOCK)
        for n, c in enumerate(spans):
            active = jnp.maximum(dot(recv[r, :width], up[:, c], NN), 0.0)
            sq[r, c] = (active * active).astype(BF16)
            act_grad = dot(recv[r, width:], down[c, :], NT)
            hid[r, c] = (act_grad * 2.0 * active).astype(BF16)
            k = i * len(spans) + n
            send_out(sq, sq_hbm, sq_sem.at[k], (r, c))
            send_out(hid, hid_hbm, hid_sem.at[k], (r, c))
        for h in range(2):
            q = slice(i * BLOCK + h * BLOCK // 2, i * BLOCK + (h + 1) * BLOCK // 2)
            ret[q, :] = dot(hid[q, :], up[...], NT).astype(BF16)
            send_out(ret, ret_hbm, ret_sem.at[2 * i + h], (q, slice(None)))
    for c in outs:
        c.wait()


def on_chip(x):
    return pltpu.with_memory_space_constraint(x, pltpu.VMEM)


def expert_pass(recv, up, down):
    total, twice = recv.shape
    width, units = up.shape
    vmem = pl.BlockSpec(memory_space=pltpu.VMEM)
    hbm = pl.BlockSpec(memory_space=pltpu.HBM)
    spans = -(-units // CHUNK)
    blocks = total // BLOCK
    dma = pltpu.SemaphoreType.DMA
    return pl.pallas_call(
        expert_kernel,
        in_specs=[vmem] * 3,
        out_specs=[hbm] * 3,
        out_shape=[
            pltpu.HBM((total, width), BF16),
            pltpu.HBM((total, units), BF16),
            pltpu.HBM((total, units), BF16),
        ],
        scratch_shapes=[
            pltpu.VMEM((total, width), BF16),
            pltpu.VMEM((total, units), BF16),
            pltpu.VMEM((total, units), BF16),
            dma((2 * blocks,)),
            dma((blocks * spans,)),
            dma((blocks * spans,)),
        ],
        compiler_params=pltpu.CompilerParams(vmem_limit_bytes=VMEM_LIMIT),
        name="expert",
    )(on_chip(recv), on_chip(up), on_chip(down))


def weight_kernel(zd_ref, sq_ref, hid_ref, up_ref, down_ref):
    width = zd_ref.shape[1] // 2
    down_ref[0] = dot(sq_ref[...], zd_ref[:, width:], TN).astype(BF16)
    up_ref[0] = dot(zd_ref[:, :width], hid_ref[...], TN).astype(BF16)


def weight_grads(zd, sq, hid):
    total, twice = zd.shape
    width, units = twice // 2, sq.shape[1]
    tile = 384
    return pl.pallas_call(
        weight_kernel,
        grid=(units // tile,),
        in_specs=[
            pl.BlockSpec((total, twice), lambda j: (0, 0)),
            pl.BlockSpec((total, tile), lambda j: (0, j)),
            pl.BlockSpec((total, tile), lambda j: (0, j)),
        ],
        out_specs=[
            pl.BlockSpec((1, width, tile), lambda j: (0, 0, j)),
            pl.BlockSpec((1, tile, width), lambda j: (0, j, 0)),
        ],
        out_shape=[
            jax.ShapeDtypeStruct((1, width, units), BF16),
            jax.ShapeDtypeStruct((1, units, width), BF16),
        ],
        compiler_params=pltpu.CompilerParams(vmem_limit_bytes=2 * VMEM_LIMIT),
        cost_estimate=pl.CostEstimate(
            flops=4 * total * width * units, transcendentals=0, bytes_accessed=8 * width * units
        ),
        name="weight_grads",
    )(zd, sq, hid)


def share_kernel(spot_ref, inputs_ref, piece_ref, keep_ref, give_ref):
    pairs, _, columns = keep_ref.shape
    acc = dot(inputs_ref[...], piece_ref[...], TN)
    core = spot_ref[0] & 1

    def emit(mine):
        for p in range(pairs):
            for half in range(2):
                at = (2 * p + half) * columns
                part = acc[:, at : at + columns]
                if half == mine:
                    keep_ref[p] = part
                else:
                    give_ref[p] = part.astype(BF16)

    @pl.when(core == 0)
    def _():
        emit(0)

    @pl.when(core == 1)
    def _():
        emit(1)


def add_kernel(spot_ref, keep_ref, got_ref, *out_refs):
    pairs = keep_ref.shape[0]
    for d, out in enumerate(out_refs):
        p = lax.rem((spot_ref[0] >> 1) + d, pairs)
        out[...] = (keep_ref[p] + got_ref[p].astype(F32)).astype(out.dtype)


def reduce_over_wide(spot, inputs, piece, n_wide):
    rows, columns = inputs.shape[1], piece.shape[1] // n_wide
    pairs = n_wide // 2
    vmem = pl.BlockSpec(memory_space=pltpu.VMEM)
    smem = pl.BlockSpec(memory_space=pltpu.SMEM)
    params = pltpu.CompilerParams(vmem_limit_bytes=VMEM_LIMIT)
    keep, give = pl.pallas_call(
        share_kernel,
        in_specs=[smem, vmem, vmem],
        out_specs=[vmem, vmem],
        out_shape=[
            pltpu.VMEM((pairs, rows, columns), F32),
            jax.ShapeDtypeStruct((pairs, rows, columns), BF16),
        ],
        compiler_params=params,
        name="share",
    )(spot, on_chip(inputs), on_chip(piece))
    got = lax.ppermute(give, "wide", [(w, w ^ 1) for w in range(n_wide)])
    own, *others = pl.pallas_call(
        add_kernel,
        in_specs=[smem, vmem, vmem],
        out_specs=[vmem] * pairs,
        out_shape=[jax.ShapeDtypeStruct((rows, columns), F32)]
        + [jax.ShapeDtypeStruct((rows, columns), BF16)] * (pairs - 1),
        compiler_params=params,
        name="add",
    )(spot, on_chip(keep), on_chip(got))
    for d, part in enumerate(others, 1):
        line = [(w, ((w >> 1) + d) % pairs * 2 + (w & 1)) for w in range(n_wide)]
        own = own + lax.ppermute(part, "wide", line).astype(F32)
    return own


def exchange(x, axes):
    return lax.all_to_all(x, axes, split_axis=0, concat_axis=0, tiled=True)


def on_device(
    latent_in, latent_grad, route_ids, gate_values, up_weight, down_weight, inputs, proj_weight
):
    n_wide = lax.axis_size("wide")
    n_narrow = lax.axis_size("narrow")
    experts = n_wide * n_narrow
    both = ("wide", "narrow")
    tokens, width = latent_in.shape
    send, place, down = pack(route_ids, gate_values, latent_in, latent_grad, down_weight[0])
    recv = exchange(send.reshape(experts, SLOTS, 2 * width), both)
    recv = recv.reshape(experts * SLOTS, 2 * width)
    rows, sq, hid = expert_pass(recv, up_weight[0], down)
    returned = exchange(rows.reshape(experts, SLOTS, width), both)
    grad_up, grad_down = weight_grads(recv, sq, hid)
    spot = lax.axis_index("wide").astype(jnp.int32).reshape(1)
    returned, grad_up, grad_down, spot = lax.optimization_barrier(
        (returned, grad_up, grad_down, spot)
    )
    token_grad = dot(place, returned.reshape(experts * SLOTS, width), NN).astype(BF16)
    copies = jnp.broadcast_to(token_grad[None], (n_narrow, tokens, width))
    piece = exchange(copies, "narrow").reshape(n_narrow * tokens, width)
    grad_proj = reduce_over_wide(spot, inputs, piece, n_wide)
    grad_inputs = dot(piece, proj_weight, NT).astype(BF16)
    return (grad_up, grad_down, grad_inputs, grad_proj)


def solution(mesh):
    placed = (
        P(("wide", "narrow"), None),
        P(("wide", "narrow"), None),
        P(("wide", "narrow"), None),
        P(("wide", "narrow"), None),
        P(("wide", "narrow"), None, None),
        P(("wide", "narrow"), None, None),
        P("wide", "narrow"),
        P("narrow", None),
    )
    return jax.shard_map(
        on_device,
        mesh=mesh,
        in_specs=placed,
        out_specs=(
            P(("wide", "narrow"), None, None),
            P(("wide", "narrow"), None, None),
            P("wide", "narrow"),
            P("narrow", "wide"),
        ),
        check_vma=False,
    )
```

```python
import functools

import jax
import jax.numpy as jnp
from jax import lax
from jax.experimental import pallas as pl
from jax.experimental.pallas import tpu as pltpu
from jax.sharding import PartitionSpec as P

BF16 = jnp.bfloat16
F32 = jnp.float32
SLOTS = 8
BLOCK = 512
CHUNK = 768
PACK_STEPS = 2
VMEM_LIMIT = 28 * 1024 * 1024


def dot(a, b, dims):
    return lax.dot_general(a, b, (dims, ((), ())), preferred_element_type=F32)


NN = ((1,), (0,))
NT = ((1,), (1,))
TN = ((0,), (0,))


def pack_kernel(
    route_hbm, gate_hbm, z_hbm, g_hbm, down_hbm,
    send, place_ref, down, route_ref, gate_ref, z_ref, g_ref, sem,
):
    pairs = ((route_hbm, route_ref), (gate_hbm, gate_ref), (z_hbm, z_ref), (g_hbm, g_ref))
    loads = [pltpu.make_async_copy(a, b, sem.at[i]) for i, (a, b) in enumerate(pairs)]
    for c in loads:
        c.start()
    fetch_down = pltpu.make_async_copy(down_hbm, down, sem.at[len(loads)])
    fetch_down.start()
    tokens, top = route_ref.shape
    experts = 128
    total, twice = send.shape
    width = twice // 2
    for c in loads:
        c.wait()
    routes = route_ref[...]
    gates = gate_ref[...]
    expert_of = lax.broadcasted_iota(jnp.int32, (tokens, experts), 1)
    hits = jnp.zeros((tokens, experts), F32)
    weights = jnp.zeros((tokens, experts), F32)
    for k in range(top):
        same = routes[:, k : k + 1] == expert_of
        hits = jnp.where(same, 1.0, hits)
        weights = jnp.where(same, gates[:, k : k + 1], weights)
    before = lax.broadcasted_iota(jnp.int32, (tokens, tokens), 1) < lax.broadcasted_iota(
        jnp.int32, (tokens, tokens), 0
    )
    rank = dot(before.astype(F32).astype(BF16), hits.astype(BF16), NN)
    rank = jnp.where(hits > 0, rank, -1.0).astype(BF16)
    terms = []
    for _ in range(3):
        terms.append(weights.astype(BF16))
        weights = weights - terms[-1].astype(F32)
    rows = total // PACK_STEPS
    for p in range(PACK_STEPS):
        r = slice(p * rows, (p + 1) * rows)
        row = lax.broadcasted_iota(jnp.int32, (rows, experts), 0) + p * rows
        expert = lax.broadcasted_iota(jnp.int32, (rows, experts), 1)
        spread_bf = jnp.where((row >> 3) == expert, 1.0, 0.0).astype(BF16)
        slot = lax.broadcasted_iota(jnp.int32, (rows, tokens), 0) & (SLOTS - 1)
        chosen = jnp.where(dot(spread_bf, rank, NT) == slot.astype(F32), 1.0, 0.0)
        gate = sum(dot(spread_bf, term, NT) for term in terms)
        gate = jnp.sum(chosen * gate, axis=1, keepdims=True)
        chosen = chosen.astype(BF16)
        send[r, :width] = dot(chosen, z_ref[...], NN).astype(BF16)
        send[r, width:] = (dot(chosen, g_ref[...], NN) * gate).astype(BF16)
        slot_t = lax.broadcasted_iota(jnp.int32, (tokens, rows), 1) & (SLOTS - 1)
        place_ref[:, r] = jnp.where(
            dot(rank, spread_bf, NT) == slot_t.astype(F32), 1.0, 0.0
        ).astype(BF16)
    fetch_down.wait()


def in_hbm(x):
    return pltpu.with_memory_space_constraint(x, pltpu.HBM)


def pack(routes, gates, z, g, down):
    tokens, width = z.shape
    total = 128 * SLOTS
    vmem = pl.BlockSpec(memory_space=pltpu.VMEM)
    return pl.pallas_call(
        pack_kernel,
        in_specs=[pl.BlockSpec(memory_space=pltpu.HBM)] * 5,
        out_specs=[vmem] * 3,
        out_shape=[
            pltpu.VMEM((total, 2 * width), BF16),
            pltpu.VMEM((tokens, total), BF16),
            pltpu.VMEM(down.shape, BF16),
        ],
        scratch_shapes=[pltpu.VMEM(x.shape, x.dtype) for x in (routes, gates, z, g)]
        + [pltpu.SemaphoreType.DMA((5,))],
        compiler_params=pltpu.CompilerParams(vmem_limit_bytes=VMEM_LIMIT),
        name="pack",
    )(*(in_hbm(x) for x in (routes, gates, z, g, down)))


def expert_kernel(
    recv, up, down, ret_hbm, sq_hbm, hid_hbm,
    ret, sq, hid, ret_sem, sq_sem, hid_sem,
):
    total, twice = recv.shape
    width = twice // 2
    edges = [*range(0, up.shape[1], CHUNK), up.shape[1]]
    spans = [slice(a, b) for a, b in zip(edges[:-1], edges[1:])]
    outs = []

    def send_out(src, dst, sem, at):
        outs.append(pltpu.make_async_copy(src.at[at], dst.at[at], sem))
        outs[-1].start()

    for i in range(total // BLOCK):
        r = slice(i * BLOCK, (i + 1) * BLOCK)
        for n, c in enumerate(spans):
            active = jnp.maximum(dot(recv[r, :width], up[:, c], NN), 0.0)
            sq[r, c] = (active * active).astype(BF16)
            act_grad = dot(recv[r, width:], down[c, :], NT)
            hid[r, c] = (act_grad * 2.0 * active).astype(BF16)
            k = i * len(spans) + n
            send_out(sq, sq_hbm, sq_sem.at[k], (r, c))
            send_out(hid, hid_hbm, hid_sem.at[k], (r, c))
        for h in range(2):
            q = slice(i * BLOCK + h * BLOCK // 2, i * BLOCK + (h + 1) * BLOCK // 2)
            ret[q, :] = dot(hid[q, :], up[...], NT).astype(BF16)
            send_out(ret, ret_hbm, ret_sem.at[2 * i + h], (q, slice(None)))
    for c in outs:
        c.wait()


def on_chip(x):
    return pltpu.with_memory_space_constraint(x, pltpu.VMEM)


def expert_pass(recv, up, down):
    total, twice = recv.shape
    width, units = up.shape
    vmem = pl.BlockSpec(memory_space=pltpu.VMEM)
    hbm = pl.BlockSpec(memory_space=pltpu.HBM)
    spans = -(-units // CHUNK)
    blocks = total // BLOCK
    dma = pltpu.SemaphoreType.DMA
    return pl.pallas_call(
        expert_kernel,
        in_specs=[vmem] * 3,
        out_specs=[hbm] * 3,
        out_shape=[
            pltpu.HBM((total, width), BF16),
            pltpu.HBM((total, units), BF16),
            pltpu.HBM((total, units), BF16),
        ],
        scratch_shapes=[
            pltpu.VMEM((total, width), BF16),
            pltpu.VMEM((total, units), BF16),
            pltpu.VMEM((total, units), BF16),
            dma((2 * blocks,)),
            dma((blocks * spans,)),
            dma((blocks * spans,)),
        ],
        compiler_params=pltpu.CompilerParams(vmem_limit_bytes=VMEM_LIMIT),
        name="expert",
    )(on_chip(recv), on_chip(up), on_chip(down))


def weight_kernel(zd_ref, sq_ref, hid_ref, up_ref, down_ref):
    width = zd_ref.shape[1] // 2
    down_ref[0] = dot(sq_ref[...], zd_ref[:, width:], TN).astype(BF16)
    up_ref[0] = dot(zd_ref[:, :width], hid_ref[...], TN).astype(BF16)


def weight_grads(zd, sq, hid):
    total, twice = zd.shape
    width, units = twice // 2, sq.shape[1]
    tile = 384
    return pl.pallas_call(
        weight_kernel,
        grid=(units // tile,),
        in_specs=[
            pl.BlockSpec((total, twice), lambda j: (0, 0)),
            pl.BlockSpec((total, tile), lambda j: (0, j)),
            pl.BlockSpec((total, tile), lambda j: (0, j)),
        ],
        out_specs=[
            pl.BlockSpec((1, width, tile), lambda j: (0, 0, j)),
            pl.BlockSpec((1, tile, width), lambda j: (0, j, 0)),
        ],
        out_shape=[
            jax.ShapeDtypeStruct((1, width, units), BF16),
            jax.ShapeDtypeStruct((1, units, width), BF16),
        ],
        compiler_params=pltpu.CompilerParams(vmem_limit_bytes=2 * VMEM_LIMIT),
        cost_estimate=pl.CostEstimate(
            flops=4 * total * width * units, transcendentals=0, bytes_accessed=8 * width * units
        ),
        name="weight_grads",
    )(zd, sq, hid)


def share_kernel(spot_ref, inputs_ref, piece_ref, keep_ref, give_ref):
    pairs, _, columns = keep_ref.shape
    acc = dot(inputs_ref[...], piece_ref[...], TN)
    core = spot_ref[0] & 1

    def emit(mine):
        for p in range(pairs):
            for half in range(2):
                at = (2 * p + half) * columns
                part = acc[:, at : at + columns]
                if half == mine:
                    keep_ref[p] = part
                else:
                    give_ref[p] = part.astype(BF16)

    @pl.when(core == 0)
    def _():
        emit(0)

    @pl.when(core == 1)
    def _():
        emit(1)


def add_kernel(spot_ref, keep_ref, got_ref, *out_refs):
    pairs = keep_ref.shape[0]
    for d, out in enumerate(out_refs):
        p = lax.rem((spot_ref[0] >> 1) + d, pairs)
        out[...] = (keep_ref[p] + got_ref[p].astype(F32)).astype(out.dtype)


def reduce_over_wide(spot, inputs, piece, n_wide):
    rows, columns = inputs.shape[1], piece.shape[1] // n_wide
    pairs = n_wide // 2
    vmem = pl.BlockSpec(memory_space=pltpu.VMEM)
    smem = pl.BlockSpec(memory_space=pltpu.SMEM)
    params = pltpu.CompilerParams(vmem_limit_bytes=VMEM_LIMIT)
    keep, give = pl.pallas_call(
        share_kernel,
        in_specs=[smem, vmem, vmem],
        out_specs=[vmem, vmem],
        out_shape=[
            pltpu.VMEM((pairs, rows, columns), F32),
            jax.ShapeDtypeStruct((pairs, rows, columns), BF16),
        ],
        compiler_params=params,
        name="share",
    )(spot, on_chip(inputs), on_chip(piece))
    got = lax.ppermute(give, "wide", [(w, w ^ 1) for w in range(n_wide)])
    own, *others = pl.pallas_call(
        add_kernel,
        in_specs=[smem, vmem, vmem],
        out_specs=[vmem] * pairs,
        out_shape=[jax.ShapeDtypeStruct((rows, columns), F32)]
        + [jax.ShapeDtypeStruct((rows, columns), BF16)] * (pairs - 1),
        compiler_params=params,
        name="add",
    )(spot, on_chip(keep), on_chip(got))
    shares = {}
    for d in sorted(range(1, pairs), key=lambda d: min(d, pairs - d)):
        line = [(w, ((w >> 1) + d) % pairs * 2 + (w & 1)) for w in range(n_wide)]
        shares[d] = lax.ppermute(others[d - 1], "wide", line)
    for d in shares:
        own = own + shares[d].astype(F32)
    return own


def exchange(x, axes):
    return lax.all_to_all(x, axes, split_axis=0, concat_axis=0, tiled=True)


def on_device(
    latent_in, latent_grad, route_ids, gate_values, up_weight, down_weight, inputs, proj_weight
):
    n_wide = lax.axis_size("wide")
    n_narrow = lax.axis_size("narrow")
    experts = n_wide * n_narrow
    both = ("wide", "narrow")
    tokens, width = latent_in.shape
    send, place, down = pack(route_ids, gate_values, latent_in, latent_grad, down_weight[0])
    recv = exchange(send.reshape(experts, SLOTS, 2 * width), both)
    recv = recv.reshape(experts * SLOTS, 2 * width)
    rows, sq, hid = expert_pass(recv, up_weight[0], down)
    returned = exchange(rows.reshape(experts, SLOTS, width), both)
    grad_up, grad_down = weight_grads(recv, sq, hid)
    spot = lax.axis_index("wide").astype(jnp.int32).reshape(1)
    returned, grad_up, grad_down, spot = lax.optimization_barrier(
        (returned, grad_up, grad_down, spot)
    )
    token_grad = dot(place, returned.reshape(experts * SLOTS, width), NN).astype(BF16)
    copies = jnp.broadcast_to(token_grad[None], (n_narrow, tokens, width))
    piece = exchange(copies, "narrow").reshape(n_narrow * tokens, width)
    grad_proj = reduce_over_wide(spot, inputs, piece, n_wide)
    grad_inputs = dot(piece, proj_weight, NT).astype(BF16)
    return (grad_up, grad_down, grad_inputs, grad_proj)


def solution(mesh):
    placed = (
        P(("wide", "narrow"), None),
        P(("wide", "narrow"), None),
        P(("wide", "narrow"), None),
        P(("wide", "narrow"), None),
        P(("wide", "narrow"), None, None),
        P(("wide", "narrow"), None, None),
        P("wide", "narrow"),
        P("narrow", None),
    )
    return jax.shard_map(
        on_device,
        mesh=mesh,
        in_specs=placed,
        out_specs=(
            P(("wide", "narrow"), None, None),
            P(("wide", "narrow"), None, None),
            P("wide", "narrow"),
            P("narrow", "wide"),
        ),
        check_vma=False,
    )
```

```python
import functools

import jax
import jax.numpy as jnp
from jax import lax
from jax.experimental import pallas as pl
from jax.experimental.pallas import tpu as pltpu
from jax.sharding import PartitionSpec as P

BF16 = jnp.bfloat16
F32 = jnp.float32
SLOTS = 8
BLOCK = 512
CHUNK = 768
PACK_STEPS = 2
VMEM_LIMIT = 28 * 1024 * 1024


def dot(a, b, dims):
    return lax.dot_general(a, b, (dims, ((), ())), preferred_element_type=F32)


NN = ((1,), (0,))
NT = ((1,), (1,))
TN = ((0,), (0,))


def pack_kernel(
    route_hbm, gate_hbm, z_hbm, g_hbm, down_hbm,
    send, place_ref, down, route_ref, gate_ref, z_ref, g_ref, sem,
):
    pairs = ((route_hbm, route_ref), (gate_hbm, gate_ref), (z_hbm, z_ref), (g_hbm, g_ref))
    loads = [pltpu.make_async_copy(a, b, sem.at[i]) for i, (a, b) in enumerate(pairs)]
    for c in loads:
        c.start()
    fetch_down = pltpu.make_async_copy(down_hbm, down, sem.at[len(loads)])
    fetch_down.start()
    tokens, top = route_ref.shape
    experts = 128
    total, twice = send.shape
    width = twice // 2
    for c in loads:
        c.wait()
    routes = route_ref[...]
    gates = gate_ref[...]
    expert_of = lax.broadcasted_iota(jnp.int32, (tokens, experts), 1)
    hits = jnp.zeros((tokens, experts), F32)
    weights = jnp.zeros((tokens, experts), F32)
    for k in range(top):
        same = routes[:, k : k + 1] == expert_of
        hits = jnp.where(same, 1.0, hits)
        weights = jnp.where(same, gates[:, k : k + 1], weights)
    before = lax.broadcasted_iota(jnp.int32, (tokens, tokens), 1) < lax.broadcasted_iota(
        jnp.int32, (tokens, tokens), 0
    )
    rank = dot(before.astype(F32).astype(BF16), hits.astype(BF16), NN)
    rank = jnp.where(hits > 0, rank, -1.0).astype(BF16)
    terms = []
    for _ in range(3):
        terms.append(weights.astype(BF16))
        weights = weights - terms[-1].astype(F32)
    rows = total // PACK_STEPS
    for p in range(PACK_STEPS):
        r = slice(p * rows, (p + 1) * rows)
        row = lax.broadcasted_iota(jnp.int32, (rows, experts), 0) + p * rows
        expert = lax.broadcasted_iota(jnp.int32, (rows, experts), 1)
        spread_bf = jnp.where((row >> 3) == expert, 1.0, 0.0).astype(BF16)
        slot = lax.broadcasted_iota(jnp.int32, (rows, tokens), 0) & (SLOTS - 1)
        chosen = jnp.where(dot(spread_bf, rank, NT) == slot.astype(F32), 1.0, 0.0)
        gate = sum(dot(spread_bf, term, NT) for term in terms)
        gate = jnp.sum(chosen * gate, axis=1, keepdims=True)
        chosen = chosen.astype(BF16)
        send[r, :width] = dot(chosen, z_ref[...], NN).astype(BF16)
        send[r, width:] = (dot(chosen, g_ref[...], NN) * gate).astype(BF16)
        slot_t = lax.broadcasted_iota(jnp.int32, (tokens, rows), 1) & (SLOTS - 1)
        place_ref[:, r] = jnp.where(
            dot(rank, spread_bf, NT) == slot_t.astype(F32), 1.0, 0.0
        ).astype(BF16)
    fetch_down.wait()


def in_hbm(x):
    return pltpu.with_memory_space_constraint(x, pltpu.HBM)


def pack(routes, gates, z, g, down):
    tokens, width = z.shape
    total = 128 * SLOTS
    vmem = pl.BlockSpec(memory_space=pltpu.VMEM)
    return pl.pallas_call(
        pack_kernel,
        in_specs=[pl.BlockSpec(memory_space=pltpu.HBM)] * 5,
        out_specs=[vmem] * 3,
        out_shape=[
            pltpu.VMEM((total, 2 * width), BF16),
            pltpu.VMEM((tokens, total), BF16),
            pltpu.VMEM(down.shape, BF16),
        ],
        scratch_shapes=[pltpu.VMEM(x.shape, x.dtype) for x in (routes, gates, z, g)]
        + [pltpu.SemaphoreType.DMA((5,))],
        compiler_params=pltpu.CompilerParams(vmem_limit_bytes=VMEM_LIMIT),
        name="pack",
    )(*(in_hbm(x) for x in (routes, gates, z, g, down)))


def expert_kernel(
    recv, up, down, ret_hbm, sq_hbm, hid_hbm, recv_hbm,
    ret, sq, hid, ret_sem, sq_sem, hid_sem, recv_sem,
):
    total, twice = recv.shape
    width = twice // 2
    edges = [*range(0, up.shape[1], CHUNK), up.shape[1]]
    spans = [slice(a, b) for a, b in zip(edges[:-1], edges[1:])]
    outs = []

    def send_out(src, dst, sem, at):
        outs.append(pltpu.make_async_copy(src.at[at], dst.at[at], sem))
        outs[-1].start()

    for i in range(total // BLOCK):
        r = slice(i * BLOCK, (i + 1) * BLOCK)
        for n, c in enumerate(spans):
            active = jnp.maximum(dot(recv[r, :width], up[:, c], NN), 0.0)
            sq[r, c] = (active * active).astype(BF16)
            act_grad = dot(recv[r, width:], down[c, :], NT)
            hid[r, c] = (act_grad * 2.0 * active).astype(BF16)
            k = i * len(spans) + n
            send_out(sq, sq_hbm, sq_sem.at[k], (r, c))
            send_out(hid, hid_hbm, hid_sem.at[k], (r, c))
        send_out(recv, recv_hbm, recv_sem.at[i], (r, slice(None)))
        for h in range(2):
            q = slice(i * BLOCK + h * BLOCK // 2, i * BLOCK + (h + 1) * BLOCK // 2)
            ret[q, :] = dot(hid[q, :], up[...], NT).astype(BF16)
            send_out(ret, ret_hbm, ret_sem.at[2 * i + h], (q, slice(None)))
    for c in outs:
        c.wait()


def on_chip(x):
    return pltpu.with_memory_space_constraint(x, pltpu.VMEM)


def expert_pass(recv, up, down):
    total, twice = recv.shape
    width, units = up.shape
    vmem = pl.BlockSpec(memory_space=pltpu.VMEM)
    hbm = pl.BlockSpec(memory_space=pltpu.HBM)
    spans = -(-units // CHUNK)
    blocks = total // BLOCK
    dma = pltpu.SemaphoreType.DMA
    return pl.pallas_call(
        expert_kernel,
        in_specs=[vmem] * 3,
        out_specs=[hbm] * 4,
        out_shape=[
            pltpu.HBM((total, width), BF16),
            pltpu.HBM((total, units), BF16),
            pltpu.HBM((total, units), BF16),
            pltpu.HBM((total, twice), BF16),
        ],
        scratch_shapes=[
            pltpu.VMEM((total, width), BF16),
            pltpu.VMEM((total, units), BF16),
            pltpu.VMEM((total, units), BF16),
            dma((2 * blocks,)),
            dma((blocks * spans,)),
            dma((blocks * spans,)),
            dma((blocks,)),
        ],
        compiler_params=pltpu.CompilerParams(vmem_limit_bytes=VMEM_LIMIT),
        name="expert",
    )(on_chip(recv), on_chip(up), on_chip(down))


def weight_kernel(zd_ref, sq_ref, hid_ref, up_ref, down_ref):
    width = zd_ref.shape[1] // 2
    down_ref[0] = dot(sq_ref[...], zd_ref[:, width:], TN).astype(BF16)
    up_ref[0] = dot(zd_ref[:, :width], hid_ref[...], TN).astype(BF16)


def weight_grads(zd, sq, hid):
    total, twice = zd.shape
    width, units = twice // 2, sq.shape[1]
    tile = 384
    return pl.pallas_call(
        weight_kernel,
        grid=(units // tile,),
        in_specs=[
            pl.BlockSpec((total, twice), lambda j: (0, 0)),
            pl.BlockSpec((total, tile), lambda j: (0, j)),
            pl.BlockSpec((total, tile), lambda j: (0, j)),
        ],
        out_specs=[
            pl.BlockSpec((1, width, tile), lambda j: (0, 0, j)),
            pl.BlockSpec((1, tile, width), lambda j: (0, j, 0)),
        ],
        out_shape=[
            jax.ShapeDtypeStruct((1, width, units), BF16),
            jax.ShapeDtypeStruct((1, units, width), BF16),
        ],
        compiler_params=pltpu.CompilerParams(vmem_limit_bytes=2 * VMEM_LIMIT),
        cost_estimate=pl.CostEstimate(
            flops=4 * total * width * units, transcendentals=0, bytes_accessed=8 * width * units
        ),
        name="weight_grads",
    )(zd, sq, hid)


def share_kernel(spot_ref, inputs_ref, piece_ref, keep_ref, give_ref):
    pairs, _, columns = keep_ref.shape
    acc = dot(inputs_ref[...], piece_ref[...], TN)
    core = spot_ref[0] & 1

    def emit(mine):
        for p in range(pairs):
            for half in range(2):
                at = (2 * p + half) * columns
                part = acc[:, at : at + columns]
                if half == mine:
                    keep_ref[p] = part
                else:
                    give_ref[p] = part.astype(BF16)

    @pl.when(core == 0)
    def _():
        emit(0)

    @pl.when(core == 1)
    def _():
        emit(1)


def add_kernel(spot_ref, keep_ref, got_ref, *out_refs):
    pairs = keep_ref.shape[0]
    for d, out in enumerate(out_refs):
        p = lax.rem((spot_ref[0] >> 1) + d, pairs)
        out[...] = (keep_ref[p] + got_ref[p].astype(F32)).astype(out.dtype)


def reduce_over_wide(spot, inputs, piece, n_wide):
    rows, columns = inputs.shape[1], piece.shape[1] // n_wide
    pairs = n_wide // 2
    vmem = pl.BlockSpec(memory_space=pltpu.VMEM)
    smem = pl.BlockSpec(memory_space=pltpu.SMEM)
    params = pltpu.CompilerParams(vmem_limit_bytes=VMEM_LIMIT)
    keep, give = pl.pallas_call(
        share_kernel,
        in_specs=[smem, vmem, vmem],
        out_specs=[vmem, vmem],
        out_shape=[
            pltpu.VMEM((pairs, rows, columns), F32),
            jax.ShapeDtypeStruct((pairs, rows, columns), BF16),
        ],
        compiler_params=params,
        name="share",
    )(spot, on_chip(inputs), on_chip(piece))
    got = lax.ppermute(give, "wide", [(w, w ^ 1) for w in range(n_wide)])
    own, *others = pl.pallas_call(
        add_kernel,
        in_specs=[smem, vmem, vmem],
        out_specs=[vmem] * pairs,
        out_shape=[jax.ShapeDtypeStruct((rows, columns), F32)]
        + [jax.ShapeDtypeStruct((rows, columns), BF16)] * (pairs - 1),
        compiler_params=params,
        name="add",
    )(spot, on_chip(keep), on_chip(got))
    for d, part in enumerate(others, 1):
        line = [(w, ((w >> 1) + d) % pairs * 2 + (w & 1)) for w in range(n_wide)]
        own = own + lax.ppermute(part, "wide", line).astype(F32)
    return own


def exchange(x, axes):
    return lax.all_to_all(x, axes, split_axis=0, concat_axis=0, tiled=True)


def on_device(
    latent_in, latent_grad, route_ids, gate_values, up_weight, down_weight, inputs, proj_weight
):
    n_wide = lax.axis_size("wide")
    n_narrow = lax.axis_size("narrow")
    experts = n_wide * n_narrow
    both = ("wide", "narrow")
    tokens, width = latent_in.shape
    send, place, down = pack(route_ids, gate_values, latent_in, latent_grad, down_weight[0])
    recv = exchange(send.reshape(experts, SLOTS, 2 * width), both)
    recv = recv.reshape(experts * SLOTS, 2 * width)
    rows, sq, hid, recv = expert_pass(recv, up_weight[0], down)
    returned = exchange(rows.reshape(experts, SLOTS, width), both)
    grad_up, grad_down = weight_grads(recv, sq, hid)
    spot = lax.axis_index("wide").astype(jnp.int32).reshape(1)
    returned, grad_up, grad_down, spot = lax.optimization_barrier(
        (returned, grad_up, grad_down, spot)
    )
    token_grad = dot(place, returned.reshape(experts * SLOTS, width), NN).astype(BF16)
    copies = jnp.broadcast_to(token_grad[None], (n_narrow, tokens, width))
    piece = exchange(copies, "narrow").reshape(n_narrow * tokens, width)
    grad_proj = reduce_over_wide(spot, inputs, piece, n_wide)
    grad_inputs = dot(piece, proj_weight, NT).astype(BF16)
    return (grad_up, grad_down, grad_inputs, grad_proj)


def solution(mesh):
    placed = (
        P(("wide", "narrow"), None),
        P(("wide", "narrow"), None),
        P(("wide", "narrow"), None),
        P(("wide", "narrow"), None),
        P(("wide", "narrow"), None, None),
        P(("wide", "narrow"), None, None),
        P("wide", "narrow"),
        P("narrow", None),
    )
    return jax.shard_map(
        on_device,
        mesh=mesh,
        in_specs=placed,
        out_specs=(
            P(("wide", "narrow"), None, None),
            P(("wide", "narrow"), None, None),
            P("wide", "narrow"),
            P("narrow", "wide"),
        ),
        check_vma=False,
    )
```
